256 devices in a mesh: tile: 32 (over y, z_hi, x), store: 8 (over z_lo, core).
Axes of the slice: x: 4, y: 4, z: 8 (z_hi: 2, z_lo: 4; z = z_hi * 4 + z_lo), core: 2. Of those that a mesh axis runs over, the one named last changes fastest.
Arguments:
- state: float32 [4, 64, 8, 4096], P(None, 'store', None, 'tile'), may hold values from -6 to 6
- cotangent: float32 [4, 64, 8, 4096], P(None, 'store', None, 'tile'), may hold values from -6 to 6
- land_mask: int32 [8, 4096], P(None, 'tile'), may hold values 0 or 1
- wet_count: int32 [8, 4096], P(None, 'tile'), may hold values from 1 to 64
- background: float32 [8, 4096], P(None, 'tile'), may hold values from 0.05 to 2
Outputs:
- state_grad: float32 [4, 64, 8, 4096], P(None, 'store', None, 'tile')
- background_grad: float32 [8, 4096], P(None, ('tile', 'store'))
The draws below stay inside these ranges and needn't reach their ends.
All inputs are finite; a program needn't handle non-finite values. No bound on the sum of `land_mask` on one device may be relied on, other than what follows from the above.
Results may differ from the reference program's by a relative error of at most 0.00002.
Values sent between devices are 32-bit elements; how exact they have to be, the bound alone decides.
A program may use at most 64 MiB of HBM per device.

```python
import math
import jax
import jax.numpy as jnp
from jax import lax

K = 64
ROWS = 8
NX = 4096


def place_ends(result, rng, low, high):
    longest = result.shape.index(max(result.shape))
    spots = []
    for shift in (0, 1):
        where = [jax.random.randint(jax.random.fold_in(rng, axis), (), 0, length) for axis, length in enumerate(result.shape)]
        where[longest] = (where[longest] + shift) % result.shape[longest]
        spots.append(tuple(where))
    return result.at[spots[0]].set(low).at[spots[1]].set(high)


def levels(own_key, shape, cuts, low, high):
    def one(position, parts):
        steps = jax.random.uniform(jax.random.fold_in(jax.random.fold_in(own_key, 6), position), (parts,), jnp.float32, low / len(cuts), high / len(cuts))
        return jnp.repeat(jnp.exp(steps), shape[position] // parts).reshape((-1,) + (1,) * (len(shape) - position - 1))

    loudness = one(*cuts[0])
    for cut in cuts[1:]:
        loudness = loudness * one(*cut)
    return loudness


def noise(rng, extent, scale, reach, pieces=(), kind=jnp.bfloat16):
    loudness = levels(rng, extent, pieces, -0.22, 0.18) if pieces else 1.0
    drawn = jax.random.normal(rng, extent, jnp.float32) * scale * loudness
    return jnp.minimum(jnp.maximum(drawn, -reach), reach).astype(kind)


def setup_inputs(seed: int = 0) -> dict:
    key_of = jax.random.split(jax.random.key(seed), 6)
    return {
        "state": noise(key_of[0], (4, K, ROWS, NX), 1.0, 6.0, ((1, 8), (3, 32)), jnp.float32),
        "cotangent": noise(key_of[1], (4, K, ROWS, NX), 1.0, 6.0, ((1, 8), (3, 32)), jnp.float32),
        "land_mask": place_ends((jax.random.randint(key_of[2], (ROWS, NX), 0, 5) < 4).astype(jnp.int32), jax.random.fold_in(key_of[2], 1), 0, 1),
        "wet_count": place_ends(jax.random.randint(key_of[3], (ROWS, NX), 1, K + 1), jax.random.fold_in(key_of[3], 1), 1, K).astype(jnp.int32),
        "background": jnp.clip(jnp.exp(math.log(2.0) - 3.6888794 * jax.random.uniform(key_of[4], (ROWS, NX), jnp.float32) ** levels(key_of[4], (ROWS, NX), ((1, 32),), -0.2, 0.2)), 0.05, 2.0),
    }


DIFFUSE = 0.1
ADVECT = 0.05
MIXING = 2.0
ALPHA_T = 0.6
BETA_S = 0.8

def wet_of(land_mask, wet_count, level_ids):
    ocean = land_mask[None] == 1
    deep = level_ids[:, None, None] < wet_count[None]
    return jnp.logical_and(ocean, deep).astype(jnp.float32)

def wrap_cols(field):
    return jnp.concatenate([field[..., -1:], field, field[..., :1]], axis=-1)

def hstep(state_pad, wet_pad):
    masked = state_pad * wet_pad
    middle = masked[..., 1:-1]
    wet_mid = wet_pad[..., 1:-1]
    eastern = masked[..., 2:]
    western = masked[..., :-2]
    wet_east = wet_pad[..., 2:]
    wet_west = wet_pad[..., :-2]
    rows_pad = ((0, 0), (0, 0), (1, 1), (0, 0))
    mid_rows = jnp.pad(middle, rows_pad)
    wet_rows = jnp.pad(wet_mid, rows_pad)
    northern = mid_rows[:, :, 2:]
    southern = mid_rows[:, :, :-2]
    wet_north = wet_rows[:, :, 2:]
    wet_south = wet_rows[:, :, :-2]
    lap = wet_east * (eastern - middle) + wet_west * (western - middle) + wet_north * (northern - middle) + wet_south * (southern - middle)
    inter = wet_mid * (middle + DIFFUSE * lap)
    zonal = middle[2]
    merid = middle[3]
    advect = -ADVECT * wet_mid[0] * (zonal * (eastern[:2] - western[:2]) + merid * (northern[:2] - southern[:2]))
    rows = state_pad.shape[2]
    latitude = 0.1 + 0.2 * (jnp.arange(rows, dtype=jnp.float32) + 0.5) / rows
    latitude = latitude[None, :, None]
    turn_u = latitude * merid
    turn_v = -latitude * zonal
    extra = jnp.concatenate([advect, turn_u[None], turn_v[None]], axis=0)
    return inter + extra

def solve_columns(upper_c, lower_c, diagonal, rhs):
    rhs_t = jnp.moveaxis(rhs, 1, 0)

    def forward(carry, item):
        ratio_prev, value_prev = carry
        upper, lower, diag_k, right = item
        pivot = diag_k - upper * ratio_prev
        ratio = lower / pivot
        value = (right + upper * value_prev) / pivot
        return ((ratio, value), (ratio, value))
    init = (jnp.zeros(upper_c.shape[1:], jnp.float32), jnp.zeros(rhs_t.shape[1:], jnp.float32))
    _, (ratios, values) = lax.scan(forward, init, (upper_c, lower_c, diagonal, rhs_t))

    def backward(carry, item):
        ratio, value = item
        solved = value + ratio * carry
        return (solved, solved)
    _, solved = lax.scan(backward, jnp.zeros(rhs_t.shape[1:], jnp.float32), (ratios, values), reverse=True)
    return jnp.moveaxis(solved, 0, 1)

def vertical(inter, tracers, cotangent, wet, background):
    density = -ALPHA_T * tracers[0] + BETA_S * tracers[1]
    wet_pair = wet[:-1] * wet[1:]
    gate = jax.nn.sigmoid(density[:-1] - density[1:])
    mix = (background[None] + MIXING * gate) * wet_pair
    zero = jnp.zeros_like(mix[:1])
    upper_c = jnp.concatenate([zero, mix], axis=0)
    lower_c = jnp.concatenate([mix, zero], axis=0)
    diagonal = 1.0 + upper_c + lower_c
    rhs = jnp.concatenate([inter, cotangent], axis=0)
    solved = solve_columns(upper_c, lower_c, diagonal, rhs)
    after = solved[:4]
    back = solved[4:]
    coef_grad = -lax.optimization_barrier(jnp.sum((back[:, :-1] - back[:, 1:]) * (after[:, :-1] - after[:, 1:]), axis=0))
    back_grad = lax.optimization_barrier(jnp.sum(coef_grad * wet_pair, axis=0))
    slope = coef_grad * MIXING * gate * (1.0 - gate) * wet_pair
    dens_grad = jnp.concatenate([slope, zero], axis=0) - jnp.concatenate([zero, slope], axis=0)
    tracer_grad = jnp.stack([-ALPHA_T * dens_grad * wet, BETA_S * dens_grad * wet], axis=0)
    return (back, tracer_grad, back_grad)

def reference(state, cotangent, land_mask, wet_count, background):
    wet = wet_of(land_mask, wet_count, jnp.arange(K, dtype=jnp.int32))
    wet_pad = wrap_cols(wet[None])
    inter = hstep(wrap_cols(state), wet_pad)
    tracers = state[:2] * wet[None]
    back, tracer_grad, back_grad = vertical(inter, tracers, cotangent, wet, background)
    _, pull = jax.vjp(lambda field: hstep(wrap_cols(field), wet_pad), state)
    grad_h, = pull(back)
    state_grad = grad_h + jnp.concatenate([tracer_grad, jnp.zeros_like(tracer_grad)], axis=0)
    return (state_grad, back_grad)
```

```python
import functools

import jax
import jax.numpy as jnp
from jax import lax
from jax.experimental import pallas as pl
from jax.experimental.pallas import tpu as pltpu
from jax.sharding import PartitionSpec as P

DIFFUSE = 0.1
ADVECT = 0.05
MIXING = 2.0
ALPHA_T = 0.6
BETA_S = 0.8
MESH = pl.DeviceIdType.MESH
F32 = jnp.float32


def lanes(x, shift):
    shift %= 128
    return pltpu.roll(x, shift, x.ndim - 1) if shift else x


def rows(x, shift):
    return pltpu.roll(x, shift % 8, x.ndim - 2)


def kernel(
    n_tile, n_store, state_h, cot_h, land_h, count_h, bg_h, out, bg_out,
    st, ct, land, count, bg,
    edge, edge_rx, bedge, bedge_rx, dens_tx, dens_rx,
    early, early_rx, ret1, ret1_rx, late, late_rx, ret2, ret2_rx, part, part_rx,
    in_sem, edge_s, edge_r, bedge_s, bedge_r, dens_s, dens_r,
    early_s, early_r, ret1_s, ret1_r, late_s, late_r, ret2_s, ret2_r, part_s, part_r,
):
    t = lax.axis_index("tile")
    s = lax.axis_index("store")
    east = lax.rem(t + 1, n_tile)
    west = lax.rem(t + n_tile - 1, n_tile)
    below = lax.rem(s + 1, n_store)
    above = lax.rem(s + n_store - 1, n_store)

    barrier = pltpu.get_barrier_semaphore()
    for d in range(1, n_store):
        pl.semaphore_signal(barrier, inc=1, device_id={"store": lax.rem(s + d, n_store)}, device_id_type=MESH)
    for to in (east, west):
        pl.semaphore_signal(barrier, inc=1, device_id={"tile": to}, device_id_type=MESH)

    loads = [
        pltpu.make_async_copy(src, dst, in_sem.at[i])
        for i, (src, dst) in enumerate(((land_h, land), (count_h, count), (bg_h, bg), (state_h, st), (cot_h, ct)))
    ]
    for load in loads:
        load.start()

    lane = lax.broadcasted_iota(jnp.int32, (8, 128), 1)
    row = lax.broadcasted_iota(jnp.int32, (8, 128), 0)
    block = lane >> 4
    pairs = ((lane + 1) & 127) >> 1
    first = lane == 0
    last = lane == 127

    def send(src, dst, send_sem, recv_sem, where):
        return pltpu.make_async_remote_copy(
            src_ref=src, dst_ref=dst, send_sem=send_sem, recv_sem=recv_sem, device_id=where, device_id_type=MESH
        )

    def mates(src, dst, send_sem, recv_sem):
        copies = []
        for d in range(1, n_store):
            to = lax.rem(s + d, n_store)
            copies.append(send(src(to), dst.at[s], send_sem.at[d - 1], recv_sem.at[d - 1], {"store": to}))
        return copies

    def start(copies):
        for copy in copies:
            copy.start()

    def arrived(copies):
        for copy in copies:
            copy.wait_recv()

    def exchange_blocks(tiles):
        tiles = list(tiles)
        for b in (4, 2, 1):
            keep = (block & b) == 0
            new = [None] * 8
            for v in range(8):
                if v & b == 0:
                    lo, hi = tiles[v], tiles[v + b]
                    new[v] = jnp.where(keep, lo, lanes(hi, 16 * b))
                    new[v + b] = jnp.where(keep, lanes(lo, -16 * b), hi)
            tiles = new
        return tiles

    def pack_edges(tiles):
        half = tiles.shape[0] // 2
        while half:
            tiles = jnp.where((pairs & half) != 0, lanes(tiles[half:], 2 * half), tiles[:half])
            half //= 2
        return tiles[0]

    def unpack_edges(from_west, from_east):
        both = lanes(jnp.where((lane & 1) == 0, from_east, lanes(from_west, 2)), 127)
        spread = both[None]
        for half in (1, 2, 4, 8, 16):
            spread = jnp.concatenate([spread, lanes(spread, -2 * half)], axis=0)
        return spread.reshape(4, 8, 8, 128), lanes(both, -64)

    def to_east(x, halo):
        return jnp.where(last, halo, lanes(x, 127))

    def to_west(x, halo):
        return jnp.where(first, halo, lanes(x, 1))

    def to_north(x):
        return jnp.where(row == 7, 0.0, rows(x, 7))

    def to_south(x):
        return jnp.where(row == 0, 0.0, rows(x, 1))

    level = (lax.broadcasted_iota(jnp.int32, (8, 8, 128), 0) + s * 8).astype(F32)
    base = (s * 8).astype(F32)

    for load in loads[:3]:
        load.wait()
    depth = jnp.where(land[...] == 1, count[...], 0).astype(F32)
    wet = jnp.where(level < depth, 1.0, 0.0)
    backgr = bg[...]

    loads[3].wait()
    masked = st[...] * wet
    edges = pack_edges(masked.reshape(32, 8, 128))
    edge[...] = jnp.where(pairs == 32, lanes(depth, 64), edges)

    density = -ALPHA_T * masked[0] + BETA_S * masked[1]
    dens_tx[0] = density[7]
    dens_tx[1] = density[0]
    gate = jax.nn.sigmoid(density[:-1] - density[1:])
    pair = wet[1:]
    mix = (backgr + MIXING * gate) * pair
    ratio = []
    inverse = []
    excess = jnp.ones((8, 128), F32)
    for i in range(8):
        if i < 7:
            inv = 1.0 / (excess + mix[i])
            ratio.append(mix[i] * inv)
            inverse.append(inv)
            excess = 1.0 + ratio[i] * excess
        else:
            inverse.append(1.0 / excess)

    def local_solve(rhs):
        values = [rhs[0] * inverse[0]]
        for i in range(1, 8):
            values.append((rhs[i] + mix[i - 1] * values[-1]) * inverse[i])
        for i in range(6, -1, -1):
            values[i] = values[i] + ratio[i] * values[i + 1]
        return values

    up = [inverse[0]]
    for i in range(1, 8):
        up.append(mix[i - 1] * up[-1] * inverse[i])
    for i in range(6, -1, -1):
        up[i] = up[i] + ratio[i] * up[i + 1]
    down = [None] * 7 + [inverse[7]]
    for i in range(6, -1, -1):
        down[i] = ratio[i] * down[i + 1]

    loads[4].wait()
    p_back = local_solve([ct[:, i] for i in range(8)])
    bottom_wet = base + 8.0 < depth
    bg_pair = jnp.where(bottom_wet, backgr, 0.0)
    ends = [p_back[0][f] for f in range(4)] + [p_back[7][f] for f in range(4)]
    for d, tile in enumerate(exchange_blocks(ends)):
        early[d, 0] = tile
    matrix = [up[0], up[7], down[7], density[0], density[7], bg_pair, bg_pair, bg_pair]
    for d, tile in enumerate(exchange_blocks(matrix)):
        early[d, 1] = tile
    early_rx[s] = early[s]

    pl.semaphore_wait(barrier, n_store - 1 + 2)
    edge_copies = [
        send(edge, edge_rx.at[0], edge_s.at[0], edge_r.at[0], {"tile": east}),
        send(edge, edge_rx.at[1], edge_s.at[1], edge_r.at[1], {"tile": west}),
    ]
    start(edge_copies)
    early_copies = mates(lambda to: early.at[to], early_rx, early_s, early_r)
    start(early_copies)
    dens_copies = [
        send(dens_tx.at[0], dens_rx.at[0], dens_s.at[0], dens_r.at[0], {"store": below}),
        send(dens_tx.at[1], dens_rx.at[1], dens_s.at[1], dens_r.at[1], {"store": above}),
    ]
    start(dens_copies)

    arrived(early_copies)
    m_inv, low, high = [], [], []
    ends_rx = [early_rx[j, 0] for j in range(8)]
    mat_rx = [early_rx[j, 1] for j in range(8)]

    def four(x):
        x = jnp.where(block == 0, x, lanes(x, 16))
        return jnp.where(block < 2, x, lanes(x, 32))

    prev = None
    for j in range(7):
        here, there = mat_rx[j], mat_rx[j + 1]
        jump = lanes(here, -64) - lanes(there, -48)
        weight = lanes(here, -80)
        m = jnp.where(weight > 0.0, weight + MIXING * jax.nn.sigmoid(jump), 0.0)
        pivot = 1.0 + m * (lanes(here, -32) + there)
        lower = m * lanes(here, -16)
        if j:
            pivot = pivot - lower * prev
        pivot = jnp.where(block == 0, pivot, 1.0)
        inv = 1.0 / pivot
        prev = m * lanes(there, -16) * inv
        m_inv.append(four(m * inv))
        low.append(four(lower * inv))
        high.append(four(prev))

    def fluxes(tiles):
        flux = []
        for j in range(7):
            value = m_inv[j] * (lanes(tiles[j], 64) - tiles[j + 1])
            flux.append(value + low[j] * flux[-1] if j else value)
        for j in range(5, -1, -1):
            flux[j] = flux[j] + high[j] * flux[j + 1]
        return flux

    def returns(flux, ref):
        left = lane < 64
        for d in range(8):
            above_flux = flux[d - 1] if d else 0.0
            below_flux = lanes(flux[d], 64) if d < 7 else 0.0
            ref[d] = jnp.where(left, above_flux, below_flux)

    returns(fluxes(ends_rx), ret1)
    ret1_rx[s] = ret1[s]
    ret1_copies = mates(lambda to: ret1.at[to], ret1_rx, ret1_s, ret1_r)
    start(ret1_copies)

    arrived(edge_copies)
    halo, depth_halo = unpack_edges(edge_rx[0], edge_rx[1])
    around = jnp.where(level < to_east(depth, depth_halo), 1.0, 0.0)
    around += jnp.where(level < to_west(depth, depth_halo), 1.0, 0.0)
    around += jnp.where(level < to_north(depth), 1.0, 0.0)
    around += jnp.where(level < to_south(depth), 1.0, 0.0)
    centre = wet * (1.0 - DIFFUSE * around)
    spread = DIFFUSE * wet
    m_east = to_east(masked, halo)
    m_west = to_west(masked, halo)
    m_north = to_north(masked)
    m_south = to_south(masked)
    latitude = 0.1 + 0.2 * (row.astype(F32) + 0.5) / 8.0
    inter = centre * masked + spread * (m_east + m_west + m_north + m_south)
    zonal, merid = masked[2], masked[3]
    grad_x = m_east[:2] - m_west[:2]
    grad_y = m_north[:2] - m_south[:2]
    advect = -ADVECT * (zonal * grad_x + merid * grad_y)
    rhs = [inter[0] + advect[0], inter[1] + advect[1], inter[2] + latitude * merid, inter[3] - latitude * zonal]
    rhs = jnp.stack(rhs, axis=1)
    p_after = local_solve([rhs[i] for i in range(8)])
    ends = [p_after[0][f] for f in range(4)] + [p_after[7][f] for f in range(4)]
    for d, tile in enumerate(exchange_blocks(ends)):
        late[d] = tile
    late_rx[s] = late[s]
    late_copies = mates(lambda to: late.at[to], late_rx, late_s, late_r)
    start(late_copies)

    arrived(ret1_copies)
    flux_b = exchange_blocks([ret1_rx[d] for d in range(8)])
    top_b = jnp.stack(flux_b[:4])
    bot_b = jnp.stack(flux_b[4:])
    back = jnp.stack([p_back[i] + up[i] * top_b - down[i] * bot_b for i in range(8)], axis=1)
    wet_back = wet * back
    bedge[...] = pack_edges(wet_back.reshape(32, 8, 128))
    bedge_copies = [
        send(bedge, bedge_rx.at[0], bedge_s.at[0], bedge_r.at[0], {"tile": east}),
        send(bedge, bedge_rx.at[1], bedge_s.at[1], bedge_r.at[1], {"tile": west}),
    ]
    start(bedge_copies)

    arrived(late_copies)
    returns(fluxes([late_rx[j] for j in range(8)]), ret2)
    ret2_rx[s] = ret2[s]
    ret2_copies = mates(lambda to: ret2.at[to], ret2_rx, ret2_s, ret2_r)
    start(ret2_copies)

    arrived(dens_copies)
    gate_top = jax.nn.sigmoid(dens_rx[0] - density[0])
    gate_bot = jax.nn.sigmoid(density[7] - dens_rx[1])
    pair_top = jnp.where(base > 0.0, wet[0], 0.0)
    pair_bot = jnp.where(bottom_wet, 1.0, 0.0)
    scale_top = pair_top / (backgr + MIXING * gate_top)
    scale_bot = pair_bot / (backgr + MIXING * gate_bot)

    arrived(ret2_copies)
    flux_a = exchange_blocks([ret2_rx[d] for d in range(8)])
    top_a = jnp.stack(flux_a[:4])
    bot_a = jnp.stack(flux_a[4:])
    after = jnp.stack([p_after[i] + up[i] * top_a - down[i] * bot_a for i in range(8)], axis=1)
    coef = -jnp.sum((back[:, :-1] - back[:, 1:]) * (after[:, :-1] - after[:, 1:]), axis=0) * pair
    coef_top = -jnp.sum(top_b * top_a, axis=0) * (scale_top * scale_top)
    coef_bot = -jnp.sum(bot_b * bot_a, axis=0) * (scale_bot * scale_bot)
    total = jnp.sum(coef, axis=0) + coef_bot
    part[...] = total
    part_rx[s] = total
    part_copies = mates(lambda to: part, part_rx, part_s, part_r)
    start(part_copies)
    slope = MIXING * coef * gate * (1.0 - gate)
    slope_top = MIXING * coef_top * gate_top * (1.0 - gate_top)
    slope_bot = MIXING * coef_bot * gate_bot * (1.0 - gate_bot)
    dens_grad = jnp.concatenate([slope, slope_bot[None]], axis=0) - jnp.concatenate([slope_top[None], slope], axis=0)

    b_north = to_north(wet_back)
    b_south = to_south(wet_back)
    arrived(bedge_copies)
    b_halo, _ = unpack_edges(bedge_rx[0], bedge_rx[1])
    b_east = to_east(wet_back, b_halo)
    b_west = to_west(wet_back, b_halo)
    grad = centre * wet_back + spread * (b_east + b_west + b_north + b_south)
    flow = m_east[2] * b_east[:2] - m_west[2] * b_west[:2] + m_north[3] * b_north[:2] - m_south[3] * b_south[:2]
    tracer = ADVECT * flow
    out[0] = grad[0] + wet * (tracer[0] - ALPHA_T * dens_grad)
    out[1] = grad[1] + wet * (tracer[1] + BETA_S * dens_grad)
    out[2] = grad[2] - ADVECT * jnp.sum(wet_back[:2] * grad_x, axis=0) - latitude * wet_back[3]
    out[3] = grad[3] - ADVECT * jnp.sum(wet_back[:2] * grad_y, axis=0) + latitude * wet_back[2]

    arrived(part_copies)
    bg_out[...] = jnp.sum(part_rx[...], axis=0)
    for copies in (edge_copies, early_copies, dens_copies, ret1_copies, late_copies, bedge_copies, ret2_copies, part_copies):
        for copy in copies:
            copy.wait_send()


def shards(n_tile, n_store, state, cotangent, land_mask, wet_count, background):
    tile = (8, 128)
    vmem = functools.partial(pltpu.VMEM, dtype=F32)
    sem = pltpu.SemaphoreType.DMA
    mates = n_store - 1
    grad, bg_sum = pl.pallas_call(
        functools.partial(kernel, n_tile, n_store),
        name="ocean",
        out_shape=(jax.ShapeDtypeStruct(state.shape, F32), jax.ShapeDtypeStruct(tile, F32)),
        in_specs=[pl.BlockSpec(memory_space=pl.ANY)] * 5,
        out_specs=(pl.BlockSpec(memory_space=pltpu.VMEM), pl.BlockSpec(memory_space=pltpu.VMEM)),
        scratch_shapes=[
            vmem(state.shape), vmem(state.shape),
            pltpu.VMEM(tile, jnp.int32), pltpu.VMEM(tile, jnp.int32), vmem(tile),
            vmem(tile), vmem((2,) + tile), vmem(tile), vmem((2,) + tile), vmem((2,) + tile), vmem((2,) + tile),
            vmem((n_store, 2) + tile), vmem((n_store, 2) + tile),
            vmem((n_store,) + tile), vmem((n_store,) + tile),
            vmem((n_store,) + tile), vmem((n_store,) + tile),
            vmem((n_store,) + tile), vmem((n_store,) + tile),
            vmem(tile), vmem((n_store,) + tile),
            sem((5,)), sem((2,)), sem((2,)), sem((2,)), sem((2,)), sem((2,)), sem((2,)),
        ] + [sem((mates,))] * 10,
        compiler_params=pltpu.CompilerParams(collective_id=0, has_side_effects=True),
    )(state, cotangent, land_mask, wet_count, background)
    part = state.shape[3] // n_store
    return grad, lax.dynamic_slice_in_dim(bg_sum, lax.axis_index("store") * part, part, 1)


def solution(mesh):
    in_specs = (
        P(None, "store", None, "tile"),
        P(None, "store", None, "tile"),
        P(None, "tile"),
        P(None, "tile"),
        P(None, "tile"),
    )
    out_specs = (P(None, "store", None, "tile"), P(None, ("tile", "store")))
    body = functools.partial(shards, mesh.shape["tile"], mesh.shape["store"])
    return jax.shard_map(body, mesh=mesh, in_specs=in_specs, out_specs=out_specs, check_vma=False)
```

```python
import functools

import jax
import jax.numpy as jnp
from jax import lax
from jax.experimental import pallas as pl
from jax.experimental.pallas import tpu as pltpu
from jax.sharding import PartitionSpec as P

DIFFUSE = 0.1
ADVECT = 0.05
MIXING = 2.0
ALPHA_T = 0.6
BETA_S = 0.8
MESH = pl.DeviceIdType.MESH
F32 = jnp.float32


def lanes(x, shift):
    shift %= 128
    return pltpu.roll(x, shift, x.ndim - 1) if shift else x


def rows(x, shift):
    return pltpu.roll(x, shift % 8, x.ndim - 2)


def kernel(
    n_tile, n_store, state_h, cot_h, land_h, count_h, bg_h, out, bg_out,
    st, ct, land, count, bg,
    edge, edge_rx, bedge, bedge_rx, dens_tx, dens_rx,
    early, early_rx, ret1, ret1_rx, late, late_rx, ret2, ret2_rx, part, part_rx,
    in_sem, edge_s, edge_r, bedge_s, bedge_r, dens_s, dens_r,
    early_s, early_r, ret1_s, ret1_r, late_s, late_r, ret2_s, ret2_r, part_s, part_r, near, far,
):
    t = lax.axis_index("tile")
    s = lax.axis_index("store")
    east = lax.rem(t + 1, n_tile)
    west = lax.rem(t + n_tile - 1, n_tile)
    below = lax.rem(s + 1, n_store)
    above = lax.rem(s + n_store - 1, n_store)

    barrier = pltpu.get_barrier_semaphore()
    core = lax.rem(s, 2)
    chip = s - core
    other = {"store": chip + 1 - core}
    for to in (east, west):
        pl.semaphore_signal(barrier, inc=1, device_id={"tile": to, "store": chip + 1}, device_id_type=MESH)
    for d in range(0, n_store, 2):
        to = lax.rem(chip + d, n_store)
        if d:
            pl.semaphore_signal(barrier, inc=1, device_id={"store": to}, device_id_type=MESH)
        else:

            @pl.when(core == 1)
            def _():
                pl.semaphore_signal(barrier, inc=1, device_id={"store": to}, device_id_type=MESH)


    loads = [
        pltpu.make_async_copy(src, dst, in_sem.at[i])
        for i, (src, dst) in enumerate(((land_h, land), (count_h, count), (bg_h, bg), (state_h, st), (cot_h, ct)))
    ]
    for load in loads:
        load.start()

    lane = lax.broadcasted_iota(jnp.int32, (8, 128), 1)
    row = lax.broadcasted_iota(jnp.int32, (8, 128), 0)
    block = lane >> 4
    pairs = ((lane + 1) & 127) >> 1
    first = lane == 0
    last = lane == 127

    def send(src, dst, send_sem, recv_sem, where):
        return pltpu.make_async_remote_copy(
            src_ref=src, dst_ref=dst, send_sem=send_sem, recv_sem=recv_sem, device_id=where, device_id_type=MESH
        )

    def mates(src, dst, send_sem, recv_sem):
        copies = []
        for d in range(1, n_store):
            to = lax.rem(s + d, n_store)
            copies.append(send(src(to), dst.at[s], send_sem.at[d - 1], recv_sem.at[d - 1], {"store": to}))
        return copies

    def start(copies):
        for copy in copies:
            copy.start()

    def arrived(copies):
        for copy in copies:
            copy.wait_recv()

    def exchange_blocks(tiles):
        tiles = list(tiles)
        for b in (4, 2, 1):
            keep = (block & b) == 0
            new = [None] * 8
            for v in range(8):
                if v & b == 0:
                    lo, hi = tiles[v], tiles[v + b]
                    new[v] = jnp.where(keep, lo, lanes(hi, 16 * b))
                    new[v + b] = jnp.where(keep, lanes(lo, -16 * b), hi)
            tiles = new
        return tiles

    def pack_edges(tiles):
        half = tiles.shape[0] // 2
        while half:
            tiles = jnp.where((pairs & half) != 0, lanes(tiles[half:], 2 * half), tiles[:half])
            half //= 2
        return tiles[0]

    def unpack_edges(from_west, from_east):
        both = lanes(jnp.where((lane & 1) == 0, from_east, lanes(from_west, 2)), 127)
        spread = both[None]
        for half in (1, 2, 4, 8, 16):
            spread = jnp.concatenate([spread, lanes(spread, -2 * half)], axis=0)
        return spread.reshape(4, 8, 8, 128), lanes(both, -64)

    def to_east(x, halo):
        return jnp.where(last, halo, lanes(x, 127))

    def to_west(x, halo):
        return jnp.where(first, halo, lanes(x, 1))

    def to_north(x):
        return jnp.where(row == 7, 0.0, rows(x, 7))

    def to_south(x):
        return jnp.where(row == 0, 0.0, rows(x, 1))

    level = (lax.broadcasted_iota(jnp.int32, (8, 8, 128), 0) + s * 8).astype(F32)
    base = (s * 8).astype(F32)

    for load in loads[:3]:
        load.wait()
    depth = jnp.where(land[...] == 1, count[...], 0).astype(F32)
    wet = jnp.where(level < depth, 1.0, 0.0)
    backgr = bg[...]

    loads[3].wait()
    masked = st[...] * wet
    edges = pack_edges(masked.reshape(32, 8, 128))
    edge[...] = jnp.where(pairs == 32, lanes(depth, 64), edges)

    density = -ALPHA_T * masked[0] + BETA_S * masked[1]
    dens_tx[0] = density[7]
    dens_tx[1] = density[0]
    gate = jax.nn.sigmoid(density[:-1] - density[1:])
    pair = wet[1:]
    mix = (backgr + MIXING * gate) * pair
    ratio = []
    inverse = []
    excess = jnp.ones((8, 128), F32)
    for i in range(8):
        if i < 7:
            inv = 1.0 / (excess + mix[i])
            ratio.append(mix[i] * inv)
            inverse.append(inv)
            excess = 1.0 + ratio[i] * excess
        else:
            inverse.append(1.0 / excess)

    def local_solve(rhs):
        values = [rhs[0] * inverse[0]]
        for i in range(1, 8):
            values.append((rhs[i] + mix[i - 1] * values[-1]) * inverse[i])
        for i in range(6, -1, -1):
            values[i] = values[i] + ratio[i] * values[i + 1]
        return values

    up = [inverse[0]]
    for i in range(1, 8):
        up.append(mix[i - 1] * up[-1] * inverse[i])
    for i in range(6, -1, -1):
        up[i] = up[i] + ratio[i] * up[i + 1]
    down = [None] * 7 + [inverse[7]]
    for i in range(6, -1, -1):
        down[i] = ratio[i] * down[i + 1]

    loads[4].wait()
    p_back = local_solve([ct[:, i] for i in range(8)])
    bottom_wet = base + 8.0 < depth
    bg_pair = jnp.where(bottom_wet, backgr, 0.0)
    ends = [p_back[0][f] for f in range(4)] + [p_back[7][f] for f in range(4)]
    for d, tile in enumerate(exchange_blocks(ends)):
        early[d, 0] = tile
    matrix = [up[0], up[7], down[7], density[0], density[7], bg_pair, bg_pair, bg_pair]
    for d, tile in enumerate(exchange_blocks(matrix)):
        early[d, 1] = tile
    early_rx[s] = early[s]

    @pl.when(core == 0)
    def _():
        pl.semaphore_wait(barrier, n_store - 1)
        pl.semaphore_signal(near, inc=1, device_id=other, device_id_type=MESH)

    @pl.when(core == 1)
    def _():
        pl.semaphore_wait(near, 1)

    early_copies = mates(lambda to: early.at[to], early_rx, early_s, early_r)
    start(early_copies)
    dens_copies = [
        send(dens_tx.at[0], dens_rx.at[0], dens_s.at[0], dens_r.at[0], {"store": below}),
        send(dens_tx.at[1], dens_rx.at[1], dens_s.at[1], dens_r.at[1], {"store": above}),
    ]
    start(dens_copies)

    @pl.when(core == 1)
    def _():
        pl.semaphore_wait(barrier, 4)
        pl.semaphore_signal(far, inc=1, device_id=other, device_id_type=MESH)

    @pl.when(core == 0)
    def _():
        pl.semaphore_wait(far, 1)

    edge_copies = [
        send(edge, edge_rx.at[0], edge_s.at[0], edge_r.at[0], {"tile": east}),
        send(edge, edge_rx.at[1], edge_s.at[1], edge_r.at[1], {"tile": west}),
    ]
    start(edge_copies)

    arrived(early_copies)
    m_inv, low, high = [], [], []
    ends_rx = [early_rx[j, 0] for j in range(8)]
    mat_rx = [early_rx[j, 1] for j in range(8)]

    def four(x):
        x = jnp.where(block == 0, x, lanes(x, 16))
        return jnp.where(block < 2, x, lanes(x, 32))

    prev = None
    for j in range(7):
        here, there = mat_rx[j], mat_rx[j + 1]
        jump = lanes(here, -64) - lanes(there, -48)
        weight = lanes(here, -80)
        m = jnp.where(weight > 0.0, weight + MIXING * jax.nn.sigmoid(jump), 0.0)
        pivot = 1.0 + m * (lanes(here, -32) + there)
        lower = m * lanes(here, -16)
        if j:
            pivot = pivot - lower * prev
        pivot = jnp.where(block == 0, pivot, 1.0)
        inv = 1.0 / pivot
        prev = m * lanes(there, -16) * inv
        m_inv.append(four(m * inv))
        low.append(four(lower * inv))
        high.append(four(prev))

    def fluxes(tiles):
        flux = []
        for j in range(7):
            value = m_inv[j] * (lanes(tiles[j], 64) - tiles[j + 1])
            flux.append(value + low[j] * flux[-1] if j else value)
        for j in range(5, -1, -1):
            flux[j] = flux[j] + high[j] * flux[j + 1]
        return flux

    def returns(flux, ref):
        left = lane < 64
        for d in range(8):
            above_flux = flux[d - 1] if d else 0.0
            below_flux = lanes(flux[d], 64) if d < 7 else 0.0
            ref[d] = jnp.where(left, above_flux, below_flux)

    returns(fluxes(ends_rx), ret1)
    ret1_rx[s] = ret1[s]
    ret1_copies = mates(lambda to: ret1.at[to], ret1_rx, ret1_s, ret1_r)
    start(ret1_copies)

    arrived(edge_copies)
    halo, depth_halo = unpack_edges(edge_rx[0], edge_rx[1])
    around = jnp.where(level < to_east(depth, depth_halo), 1.0, 0.0)
    around += jnp.where(level < to_west(depth, depth_halo), 1.0, 0.0)
    around += jnp.where(level < to_north(depth), 1.0, 0.0)
    around += jnp.where(level < to_south(depth), 1.0, 0.0)
    centre = wet * (1.0 - DIFFUSE * around)
    spread = DIFFUSE * wet
    m_east = to_east(masked, halo)
    m_west = to_west(masked, halo)
    m_north = to_north(masked)
    m_south = to_south(masked)
    latitude = 0.1 + 0.2 * (row.astype(F32) + 0.5) / 8.0
    inter = centre * masked + spread * (m_east + m_west + m_north + m_south)
    zonal, merid = masked[2], masked[3]
    grad_x = m_east[:2] - m_west[:2]
    grad_y = m_north[:2] - m_south[:2]
    advect = -ADVECT * (zonal * grad_x + merid * grad_y)
    rhs = [inter[0] + advect[0], inter[1] + advect[1], inter[2] + latitude * merid, inter[3] - latitude * zonal]
    rhs = jnp.stack(rhs, axis=1)
    p_after = local_solve([rhs[i] for i in range(8)])
    ends = [p_after[0][f] for f in range(4)] + [p_after[7][f] for f in range(4)]
    for d, tile in enumerate(exchange_blocks(ends)):
        late[d] = tile
    late_rx[s] = late[s]
    late_copies = mates(lambda to: late.at[to], late_rx, late_s, late_r)
    start(late_copies)

    arrived(ret1_copies)
    flux_b = exchange_blocks([ret1_rx[d] for d in range(8)])
    top_b = jnp.stack(flux_b[:4])
    bot_b = jnp.stack(flux_b[4:])
    back = jnp.stack([p_back[i] + up[i] * top_b - down[i] * bot_b for i in range(8)], axis=1)
    wet_back = wet * back
    bedge[...] = pack_edges(wet_back.reshape(32, 8, 128))
    bedge_copies = [
        send(bedge, bedge_rx.at[0], bedge_s.at[0], bedge_r.at[0], {"tile": east}),
        send(bedge, bedge_rx.at[1], bedge_s.at[1], bedge_r.at[1], {"tile": west}),
    ]
    start(bedge_copies)

    arrived(late_copies)
    returns(fluxes([late_rx[j] for j in range(8)]), ret2)
    ret2_rx[s] = ret2[s]
    ret2_copies = mates(lambda to: ret2.at[to], ret2_rx, ret2_s, ret2_r)
    start(ret2_copies)

    arrived(dens_copies)
    gate_top = jax.nn.sigmoid(dens_rx[0] - density[0])
    gate_bot = jax.nn.sigmoid(density[7] - dens_rx[1])
    pair_top = jnp.where(base > 0.0, wet[0], 0.0)
    pair_bot = jnp.where(bottom_wet, 1.0, 0.0)
    scale_top = pair_top / (backgr + MIXING * gate_top)
    scale_bot = pair_bot / (backgr + MIXING * gate_bot)

    arrived(ret2_copies)
    flux_a = exchange_blocks([ret2_rx[d] for d in range(8)])
    top_a = jnp.stack(flux_a[:4])
    bot_a = jnp.stack(flux_a[4:])
    after = jnp.stack([p_after[i] + up[i] * top_a - down[i] * bot_a for i in range(8)], axis=1)
    coef = -jnp.sum((back[:, :-1] - back[:, 1:]) * (after[:, :-1] - after[:, 1:]), axis=0) * pair
    coef_top = -jnp.sum(top_b * top_a, axis=0) * (scale_top * scale_top)
    coef_bot = -jnp.sum(bot_b * bot_a, axis=0) * (scale_bot * scale_bot)
    total = jnp.sum(coef, axis=0) + coef_bot
    part[...] = total
    part_rx[s] = total
    part_copies = mates(lambda to: part, part_rx, part_s, part_r)
    start(part_copies)
    slope = MIXING * coef * gate * (1.0 - gate)
    slope_top = MIXING * coef_top * gate_top * (1.0 - gate_top)
    slope_bot = MIXING * coef_bot * gate_bot * (1.0 - gate_bot)
    dens_grad = jnp.concatenate([slope, slope_bot[None]], axis=0) - jnp.concatenate([slope_top[None], slope], axis=0)

    b_north = to_north(wet_back)
    b_south = to_south(wet_back)
    arrived(bedge_copies)
    b_halo, _ = unpack_edges(bedge_rx[0], bedge_rx[1])
    b_east = to_east(wet_back, b_halo)
    b_west = to_west(wet_back, b_halo)
    grad = centre * wet_back + spread * (b_east + b_west + b_north + b_south)
    flow = m_east[2] * b_east[:2] - m_west[2] * b_west[:2] + m_north[3] * b_north[:2] - m_south[3] * b_south[:2]
    tracer = ADVECT * flow
    out[0] = grad[0] + wet * (tracer[0] - ALPHA_T * dens_grad)
    out[1] = grad[1] + wet * (tracer[1] + BETA_S * dens_grad)
    out[2] = grad[2] - ADVECT * jnp.sum(wet_back[:2] * grad_x, axis=0) - latitude * wet_back[3]
    out[3] = grad[3] - ADVECT * jnp.sum(wet_back[:2] * grad_y, axis=0) + latitude * wet_back[2]

    arrived(part_copies)
    bg_out[...] = jnp.sum(part_rx[...], axis=0)
    for copies in (edge_copies, early_copies, dens_copies, ret1_copies, late_copies, bedge_copies, ret2_copies, part_copies):
        for copy in copies:
            copy.wait_send()


def shards(n_tile, n_store, state, cotangent, land_mask, wet_count, background):
    tile = (8, 128)
    vmem = functools.partial(pltpu.VMEM, dtype=F32)
    sem = pltpu.SemaphoreType.DMA
    mates = n_store - 1
    grad, bg_sum = pl.pallas_call(
        functools.partial(kernel, n_tile, n_store),
        name="ocean",
        out_shape=(jax.ShapeDtypeStruct(state.shape, F32), jax.ShapeDtypeStruct(tile, F32)),
        in_specs=[pl.BlockSpec(memory_space=pl.ANY)] * 5,
        out_specs=(pl.BlockSpec(memory_space=pltpu.VMEM), pl.BlockSpec(memory_space=pltpu.VMEM)),
        scratch_shapes=[
            vmem(state.shape), vmem(state.shape),
            pltpu.VMEM(tile, jnp.int32), pltpu.VMEM(tile, jnp.int32), vmem(tile),
            vmem(tile), vmem((2,) + tile), vmem(tile), vmem((2,) + tile), vmem((2,) + tile), vmem((2,) + tile),
            vmem((n_store, 2) + tile), vmem((n_store, 2) + tile),
            vmem((n_store,) + tile), vmem((n_store,) + tile),
            vmem((n_store,) + tile), vmem((n_store,) + tile),
            vmem((n_store,) + tile), vmem((n_store,) + tile),
            vmem(tile), vmem((n_store,) + tile),
            sem((5,)), sem((2,)), sem((2,)), sem((2,)), sem((2,)), sem((2,)), sem((2,)),
        ] + [sem((mates,))] * 10 + [pltpu.SemaphoreType.REGULAR] * 2,
        compiler_params=pltpu.CompilerParams(collective_id=0, has_side_effects=True),
    )(state, cotangent, land_mask, wet_count, background)
    part = state.shape[3] // n_store
    return grad, lax.dynamic_slice_in_dim(bg_sum, lax.axis_index("store") * part, part, 1)


def solution(mesh):
    in_specs = (
        P(None, "store", None, "tile"),
        P(None, "store", None, "tile"),
        P(None, "tile"),
        P(None, "tile"),
        P(None, "tile"),
    )
    out_specs = (P(None, "store", None, "tile"), P(None, ("tile", "store")))
    body = functools.partial(shards, mesh.shape["tile"], mesh.shape["store"])
    return jax.shard_map(body, mesh=mesh, in_specs=in_specs, out_specs=out_specs, check_vma=False)
```

```python
import functools

import jax
import jax.numpy as jnp
from jax import lax
from jax.experimental import pallas as pl
from jax.experimental.pallas import tpu as pltpu
from jax.sharding import PartitionSpec as P

DIFFUSE = 0.1
ADVECT = 0.05
MIXING = 2.0
ALPHA_T = 0.6
BETA_S = 0.8
MESH = pl.DeviceIdType.MESH
F32 = jnp.float32


def lanes(x, shift):
    shift %= 128
    return pltpu.roll(x, shift, x.ndim - 1) if shift else x


def rows(x, shift):
    return pltpu.roll(x, shift % 8, x.ndim - 2)


def kernel(
    n_tile, n_store, state_h, cot_h, land_h, count_h, bg_h, out, bg_out,
    st, ct, land, count, bg,
    xa, xb, halo_rx, far_rx, own_rx, dens_tx, dens_rx,
    early, early_rx, ret1, ret1_rx, ret2, ret2_rx, part, part_rx, edge_bg,
    in_sem, halo_s, halo_r, far_s, far_r, own_s, own_r, dens_s, dens_r,
    early_s, early_r, ret1_s, ret1_r, ret2_s, ret2_r, part_s, part_r, near, far,
):
    t = lax.axis_index("tile")
    s = lax.axis_index("store")
    east = lax.rem(t + 1, n_tile)
    west = lax.rem(t + n_tile - 1, n_tile)
    below = lax.rem(s + 1, n_store)
    above = lax.rem(s + n_store - 1, n_store)
    end = n_store - 1
    owner = jnp.logical_or(s == 0, s == end)
    late = lax.rem(t // 4, 2) == 1

    barrier = pltpu.get_barrier_semaphore()

    def greet(**where):
        pl.semaphore_signal(barrier, inc=1, device_id=where, device_id_type=MESH)

    core = lax.rem(s, 2)
    chip = s - core
    other = {"store": chip + 1 - core}
    for to in (east, west):
        greet(tile=to, store=chip + 1)
    greet(**other)
    for d in range(2, n_store, 2):
        greet(store=lax.rem(chip + d, n_store))

    @pl.when(s == 0)
    def _():
        for d in range(1, n_store, 2):
            greet(tile=west, store=d)

    @pl.when(s == end)
    def _():
        for d in range(1, n_store, 2):
            greet(tile=east, store=d)

    loads = [
        pltpu.make_async_copy(src, dst, in_sem.at[i])
        for i, (src, dst) in enumerate(((land_h, land), (count_h, count), (bg_h, bg), (state_h, st), (cot_h, ct)))
    ]
    for load in loads:
        load.start()

    lane = lax.broadcasted_iota(jnp.int32, (8, 128), 1)
    row = lax.broadcasted_iota(jnp.int32, (8, 128), 0)
    block = lane >> 4
    field = (lane & 15) >> 1
    even = (lane & 1) == 0
    pairs = ((lane + 1) & 127) >> 1
    first = lane == 0
    last = lane == 127
    edge = jnp.logical_or(first, last)

    def send(src, dst, send_sem, recv_sem, where):
        return pltpu.make_async_remote_copy(
            src_ref=src, dst_ref=dst, send_sem=send_sem, recv_sem=recv_sem, device_id=where, device_id_type=MESH
        )

    def mates(src, dst, send_sem, recv_sem):
        copies = []
        for d in range(1, n_store):
            to = lax.rem(s + d, n_store)
            copies.append(send(src(to), dst.at[s], send_sem.at[d - 1], recv_sem.at[d - 1], {"store": to}))
        return copies

    def start(copies):
        for copy in copies:
            copy.start()

    def arrived(copies):
        for copy in copies:
            copy.wait_recv()

    def exchange_blocks(tiles):
        tiles = list(tiles)
        for b in (4, 2, 1):
            keep = (block & b) == 0
            new = [None] * 8
            for v in range(8):
                if v & b == 0:
                    lo, hi = tiles[v], tiles[v + b]
                    new[v] = jnp.where(keep, lo, lanes(hi, 16 * b))
                    new[v + b] = jnp.where(keep, lanes(lo, -16 * b), hi)
            tiles = new
        return tiles

    def pack_edges(tiles, bits):
        for bit in bits:
            half = tiles.shape[0] // 2
            tiles = jnp.where((pairs & bit) != 0, lanes(tiles[half:], 2 * bit), tiles[:half])
        return jnp.where(even, tiles[0], lanes(tiles[0], 2))

    def column(x, c):
        return jnp.broadcast_to(x[:, c : c + 1], (8, 128))

    def to_north(x):
        return jnp.where(row == 7, 0.0, rows(x, 7))

    def to_south(x):
        return jnp.where(row == 0, 0.0, rows(x, 1))

    def eliminate(mix):
        ratio, inverse = [], []
        excess = jnp.ones((8, 128), F32)
        for i in range(7):
            inv = 1.0 / (excess + mix[i])
            ratio.append(mix[i] * inv)
            inverse.append(inv)
            excess = 1.0 + ratio[i] * excess
        inverse.append(1.0 / excess)
        up = [inverse[0]]
        for i in range(1, 8):
            up.append(mix[i - 1] * up[-1] * inverse[i])
        for i in range(6, -1, -1):
            up[i] = up[i] + ratio[i] * up[i + 1]
        down = [None] * 7 + [inverse[7]]
        for i in range(6, -1, -1):
            down[i] = ratio[i] * down[i + 1]
        return (mix, ratio, inverse), up, down

    def local_solve(system, rhs):
        mix, ratio, inverse = system
        values = [rhs[0] * inverse[0]]
        for i in range(1, 8):
            values.append((rhs[i] + mix[i - 1] * values[-1]) * inverse[i])
        for i in range(6, -1, -1):
            values[i] = values[i] + ratio[i] * values[i + 1]
        return values

    def edge_system(tiles, start_level, depths, backs):
        dens = -ALPHA_T * tiles + BETA_S * lanes(tiles, -2)
        for bit in (1, 2, 4):
            dens = jnp.where((field & bit) == 0, dens, lanes(dens, 2 * bit))
        wets = jnp.where(jnp.stack([start_level + i for i in range(8)]) < depths, 1.0, 0.0)
        mixes = (backs + MIXING * jax.nn.sigmoid(dens[:-1] - dens[1:])) * wets[1:]
        return dens, wets, eliminate(mixes)

    def reduce_blocks(tiles):
        m_all, m_inv, low, high = [], [], [], []
        for j in range(7):
            here, there = tiles[j], tiles[j + 1]
            weight = lanes(here, -80)
            gates = jax.nn.sigmoid(lanes(here, -64) - lanes(there, -48))
            m = jnp.where(weight > 0.0, weight + MIXING * gates, 0.0)
            pivot = 1.0 + m * (lanes(here, -32) + there)
            lower = m * lanes(here, -16)
            if j:
                pivot = pivot - lower * high[-1]
            inv = 1.0 / jnp.where(block == 0, pivot, 1.0)
            m_all.append(m)
            m_inv.append(m * inv)
            low.append(lower * inv)
            high.append(m * lanes(there, -16) * inv)
        return m_all, m_inv, low, high

    def fluxes(m_inv, low, high, jumps):
        flux = []
        for j in range(7):
            value = m_inv[j] * jumps[j]
            flux.append(value + low[j] * flux[-1] if j else value)
        for j in range(5, -1, -1):
            flux[j] = flux[j] + high[j] * flux[j + 1]
        return flux

    level = (lax.broadcasted_iota(jnp.int32, (8, 8, 128), 0) + s * 8).astype(F32)
    base = (s * 8).astype(F32)

    for load in loads:
        load.wait()
    depth = jnp.where(land[...] == 1, count[...], 0).astype(F32)
    wet = jnp.where(level < depth, 1.0, 0.0)
    backgr = bg[...]
    masked = st[...] * wet
    xa[0] = jnp.where(jnp.logical_or(lane < 32, lane >= 96), depth, lanes(backgr, 64))
    fields = [masked[f] for f in range(4)] + [ct[f] for f in range(4)]
    own_edges = pack_edges(jnp.stack([fields[f][i] for i in range(8) for f in range(8)]), (32, 16, 8, 4, 2, 1))
    xa[1] = own_edges
    xb[0] = own_edges

    far_copies = [
        send(xa, far_rx.at[s], far_s.at[0], far_r.at[s], {"tile": east, "store": 0}),
        send(xa, far_rx.at[s], far_s.at[1], far_r.at[s], {"tile": west, "store": end}),
        send(xa, halo_rx.at[0], halo_s.at[0], halo_r.at[0], {"tile": east}),
        send(xa, halo_rx.at[1], halo_s.at[1], halo_r.at[1], {"tile": west}),
    ]

    def to_neighbours():
        @pl.when(core == 1)
        def _():
            pl.semaphore_wait(barrier, 7)
            pl.semaphore_signal(far, inc=1, device_id=other, device_id_type=MESH)

        @pl.when(core == 0)
        def _():
            pl.semaphore_wait(far, 1)

        start(far_copies)

    pl.when(late)(to_neighbours)

    density = -ALPHA_T * masked[0] + BETA_S * masked[1]
    dens_tx[0] = density[7]
    dens_tx[1] = density[0]
    gate = jax.nn.sigmoid(density[:-1] - density[1:])
    pair = wet[1:]
    system, up, down = eliminate((backgr + MIXING * gate) * pair)
    p_back = local_solve(system, [ct[:, i] for i in range(8)])

    shift_e = jnp.where(last, 0.0, lanes(masked, 127))
    shift_w = jnp.where(first, 0.0, lanes(masked, 1))
    around = jnp.where(level < jnp.where(last, 0.0, lanes(depth, 127)), 1.0, 0.0)
    around += jnp.where(level < jnp.where(first, 0.0, lanes(depth, 1)), 1.0, 0.0)
    around += jnp.where(level < to_north(depth), 1.0, 0.0)
    around += jnp.where(level < to_south(depth), 1.0, 0.0)
    centre = wet * (1.0 - DIFFUSE * around)
    spread = DIFFUSE * wet
    m_north = to_north(masked)
    m_south = to_south(masked)
    latitude = 0.1 + 0.2 * (row.astype(F32) + 0.5) / 8.0
    inter = centre * masked + spread * (shift_e + shift_w + m_north + m_south)
    zonal, merid = masked[2], masked[3]
    grad_x = shift_e[:2] - shift_w[:2]
    grad_y = m_north[:2] - m_south[:2]
    advect = -ADVECT * (zonal * grad_x + merid * grad_y)
    inter = [inter[0] + advect[0], inter[1] + advect[1], inter[2] + latitude * merid, inter[3] - latitude * zonal]
    xb[1] = pack_edges(jnp.stack([inter[f][i] for i in range(8) for f in range(4)]), (32, 16, 8, 2, 1))
    inter = jnp.stack(inter)
    p_after = local_solve(system, [inter[:, i] for i in range(8)])

    bottom_wet = base + 8.0 < depth
    bg_pair = jnp.where(bottom_wet, backgr, 0.0)
    groups = (
        [p_back[0][f] for f in range(4)] + [p_back[7][f] for f in range(4)],
        [p_after[0][f] for f in range(4)] + [p_after[7][f] for f in range(4)],
        [up[0], up[7], down[7], density[0], density[7], bg_pair, bg_pair, bg_pair],
    )
    for g, group in enumerate(groups):
        for d, tile in enumerate(exchange_blocks(group)):
            early[d, g] = tile
    early_rx[s] = early[s]
    own_rx[s] = xb[...]

    @pl.when(core == 0)
    def _():
        pl.semaphore_wait(barrier, end)
        pl.semaphore_signal(near, inc=1, device_id=other, device_id_type=MESH)

    @pl.when(core == 1)
    def _():
        pl.semaphore_wait(near, 1)

    early_copies = mates(lambda to: early.at[to], early_rx, early_s, early_r)
    start(early_copies)
    dens_copies = [
        send(dens_tx.at[0], dens_rx.at[0], dens_s.at[0], dens_r.at[0], {"store": below}),
        send(dens_tx.at[1], dens_rx.at[1], dens_s.at[1], dens_r.at[1], {"store": above}),
    ]
    start(dens_copies)
    own_copies = [
        (to, send(xb, own_rx.at[s], own_s.at[k], own_r.at[s], {"store": to})) for k, to in enumerate((0, end))
    ]
    for to, copy in own_copies:
        pl.when(s != to)(copy.start)

    pl.when(jnp.logical_not(late))(to_neighbours)

    arrived(early_copies)
    _, *coefs = reduce_blocks([early_rx[j, 2] for j in range(8)])

    def four(x):
        x = jnp.where(block == 0, x, lanes(x, 16))
        return jnp.where(block < 2, x, lanes(x, 32))

    coefs = [[four(x) for x in xs] for xs in coefs]
    left = lane < 64
    for g in range(2):
        ends = [early_rx[j, g] for j in range(8)]
        flux = fluxes(*coefs, [lanes(ends[j], 64) - ends[j + 1] for j in range(7)])
        for d in range(8):
            above_flux = flux[d - 1] if d else 0.0
            below_flux = lanes(flux[d], 64) if d < 7 else 0.0
            ret1[d, g] = jnp.where(left, above_flux, below_flux)
    ret1_rx[s] = ret1[s]
    ret1_copies = mates(lambda to: ret1.at[to], ret1_rx, ret1_s, ret1_r)
    start(ret1_copies)

    arrived(dens_copies)
    gate_top = jax.nn.sigmoid(dens_rx[0] - density[0])
    gate_bot = jax.nn.sigmoid(density[7] - dens_rx[1])
    pair_top = jnp.where(base > 0.0, wet[0], 0.0)
    pair_bot = jnp.where(bottom_wet, 1.0, 0.0)
    scale_top = pair_top / (backgr + MIXING * gate_top)
    scale_bot = pair_bot / (backgr + MIXING * gate_bot)

    def coefficients(after, top_a, bot_a):
        coef = -jnp.sum(diff_b * (after[:, :-1] - after[:, 1:]), axis=0) * pair
        coef_top = -jnp.sum(top_b * top_a, axis=0) * (scale_top * scale_top)
        coef_bot = -jnp.sum(bot_b * bot_a, axis=0) * (scale_bot * scale_bot)
        return coef, coef_top, coef_bot

    def finish(p, top, bot):
        return jnp.stack([p[i] + up[i] * top - down[i] * bot for i in range(8)], axis=1)

    arrived(ret1_copies)
    flux_b = exchange_blocks([ret1_rx[d, 0] for d in range(8)])
    flux_a = exchange_blocks([ret1_rx[d, 1] for d in range(8)])
    top_b, bot_b = jnp.stack(flux_b[:4]), jnp.stack(flux_b[4:])
    top_a, bot_a = jnp.stack(flux_a[:4]), jnp.stack(flux_a[4:])
    back = finish(p_back, top_b, bot_b)
    diff_b = back[:, :-1] - back[:, 1:]
    coef, _, coef_bot = coefficients(finish(p_after, top_a, bot_a), top_a, bot_a)
    total = jnp.sum(coef, axis=0) + coef_bot
    part[...] = total
    part_rx[s] = total
    part_copies = mates(lambda to: part, part_rx, part_s, part_r)
    start(part_copies)

    mine = lax.rem(s, 2)
    ret2_copies = [
        send(ret2.at[lax.rem(s + d, n_store)], ret2_rx.at[mine], ret2_s.at[d - 1], ret2_r.at[mine],
             {"store": lax.rem(s + d, n_store)})
        for d in range(1, n_store)
    ]

    @pl.when(owner)
    def _():
        for d in range(1, n_store):
            src = lax.rem(s + d, n_store)
            send(xb, own_rx.at[src], own_s.at[0], own_r.at[src], {"store": src}).wait_recv()
        for src in range(n_store):
            send(xa, far_rx.at[src], far_s.at[0], far_r.at[src], {"tile": east}).wait_recv()
        is_own = (lane & 1) == mine
        own = exchange_blocks([own_rx[j, 0] for j in range(8)])
        inter0 = jnp.stack(exchange_blocks([own_rx[j, 1] for j in range(8)]))
        halo = exchange_blocks([far_rx[j, 1] for j in range(8)])
        both = jnp.stack([jnp.where(is_own, own[i], halo[i]) for i in range(8)])
        there = far_rx[0, 0]

        def sides(x, a, b):
            return jnp.where(even, column(x, a), column(x, b))

        depths = jnp.where(is_own, sides(depth, 0, 127), sides(there, 0, 127))
        backs = jnp.where(is_own, sides(backgr, 0, 127), sides(there, 64, 63))
        start_level = (block * 8).astype(F32)
        dens, wets, (edge_sys, e_up, e_down) = edge_system(both, start_level, depths, backs)

        def swap(x):
            return jnp.where(even, lanes(x, -1), lanes(x, 1))

        m_halo = swap(both)
        along = jnp.where(field == 0, lanes(both, -4), lanes(both, -2)) * jnp.where(even, ADVECT, -ADVECT)
        delta = DIFFUSE * wets * (m_halo - swap(wets) * both) + jnp.where(field < 2, along * m_halo, 0.0)
        rhs = jnp.where(field < 4, jnp.where(is_own, inter0 + delta, 0.0), both)
        p = local_solve(edge_sys, [rhs[i] for i in range(8)])
        weight = jnp.where(start_level + 8.0 < depths, backs, 0.0)
        blocks = exchange_blocks([e_up[0], e_up[7], e_down[7], dens[0], dens[7], weight, p[0], p[7]])
        m_all, *e_coefs = reduce_blocks(blocks)
        flux = fluxes(*e_coefs, [lanes(blocks[j], -112) - lanes(blocks[j + 1], -96) for j in range(7)])
        for d in range(8):
            above_flux = flux[d - 1] if d else 0.0
            below_flux = lanes(flux[d], 16) if d < 7 else 0.0
            ret2[d] = jnp.where(block == 0, above_flux, jnp.where(block == 1, below_flux, 0.0))
        ret2_rx[mine] = ret2[s]
        start(ret2_copies)

        top = jnp.zeros((8, 128), F32)
        bot = jnp.zeros((8, 128), F32)
        for j in range(7):
            top = jnp.where(block == j + 1, lanes(flux[j], 16 * (j + 1)), top)
            bot = jnp.where(block == j, lanes(flux[j], 16 * j), bot)
        x = jnp.stack([p[i] + e_up[i] * top - e_down[i] * bot for i in range(8)])
        diff = x[:-1] - x[1:]
        result = jnp.sum(wets[1:] * diff * lanes(diff, -8), axis=0)
        for shift in (64, 32, 16):
            result = result + lanes(result, shift)
        for j in range(7):
            jump = jnp.where(m_all[j] > 0.0, flux[j] / m_all[j], 0.0)
            result = result + jump * lanes(jump, -8)
        result = result + lanes(result, -2)
        result = -(result + lanes(result, -4))
        edge_bg[...] = jnp.where(first, result, lanes(result, 126))

    wet_back = wet * back
    b_east = jnp.where(last, 0.0, lanes(wet_back, 127))
    b_west = jnp.where(first, 0.0, lanes(wet_back, 1))
    b_north = to_north(wet_back)
    b_south = to_south(wet_back)
    grad = centre * wet_back + spread * (b_east + b_west + b_north + b_south)
    flow = shift_e[2] * b_east[:2] - shift_w[2] * b_west[:2] + m_north[3] * b_north[:2] - m_south[3] * b_south[:2]
    grad_t = grad[:2] + ADVECT * wet * flow
    grad_u = grad[2] - ADVECT * jnp.sum(wet_back[:2] * grad_x, axis=0) - latitude * wet_back[3]
    grad_v = grad[3] - ADVECT * jnp.sum(wet_back[:2] * grad_y, axis=0) + latitude * wet_back[2]

    arrived(far_copies[2:])
    from_west, from_east = halo_rx[0], halo_rx[1]
    cols = jnp.where(even, from_east[1], from_west[1])
    cols = jnp.stack([lanes(cols, -16 * i) for i in range(8)])
    depths = jnp.where(even, column(from_east[0], 0), column(from_west[0], 127))
    backs = jnp.where(even, column(from_east[0], 64), column(from_west[0], 63))
    _, h_wet, (h_sys, h_up, h_down) = edge_system(cols, jnp.full((8, 128), base), depths, backs)
    p_halo = local_solve(h_sys, [cols[i] for i in range(8)])
    m_halo = jnp.stack([lanes(cols, 127 - 2 * f) for f in range(4)])
    depth_halo = jnp.where(last, column(from_east[0], 0), column(from_west[0], 127))
    edge_wet = jnp.where(jnp.logical_and(edge, level < depth_halo), wet, 0.0)
    sign = jnp.where(last, ADVECT, jnp.where(first, -ADVECT, 0.0))
    m_edge = jnp.where(edge, m_halo, 0.0)
    delta = spread * m_edge - DIFFUSE * edge_wet * masked
    delta_t = delta[:2] - sign * zonal * m_edge[:2]
    delta = inter + jnp.concatenate([delta_t, delta[2:]], axis=0)
    p_after = local_solve(system, [delta[:, i] for i in range(8)])
    grad_t = grad_t - DIFFUSE * edge_wet * wet_back[:2]
    grad_u = grad_u - DIFFUSE * edge_wet * wet_back[2] - sign * jnp.sum(wet_back[:2] * m_edge[:2], axis=0)
    grad_v = grad_v - DIFFUSE * edge_wet * wet_back[3]

    for k, to in enumerate((0, end)):

        @pl.when(s != to)
        def _():
            send(ret2.at[0], ret2_rx.at[k], ret2_s.at[0], ret2_r.at[k], {"store": to}).wait_recv()

    west_edge, east_edge = ret2_rx[0], ret2_rx[1]
    own = jnp.where(even, west_edge, lanes(east_edge, -2))
    top_a = jnp.where(edge, jnp.stack([lanes(own, -2 * f) for f in range(4)]), top_a)
    bot_a = jnp.where(edge, jnp.stack([lanes(own, -2 * f - 16) for f in range(4)]), bot_a)
    coef, coef_top, coef_bot = coefficients(finish(p_after, top_a, bot_a), top_a, bot_a)
    slope = MIXING * coef * gate * (1.0 - gate)
    slope_top = MIXING * coef_top * gate_top * (1.0 - gate_top)
    slope_bot = MIXING * coef_bot * gate_bot * (1.0 - gate_bot)
    dens_grad = jnp.concatenate([slope, slope_bot[None]], axis=0) - jnp.concatenate([slope_top[None], slope], axis=0)

    h_flux = jnp.where(even, east_edge, west_edge)
    h_bot = lanes(h_flux, -16)
    h_back = h_wet * jnp.stack([p_halo[i] + h_up[i] * h_flux - h_down[i] * h_bot for i in range(8)])
    b_edge = jnp.where(edge, jnp.stack([lanes(h_back, 119 - 2 * f) for f in range(4)]), 0.0)
    flow = sign * m_edge[2]
    add = spread * b_edge
    out[0] = grad_t[0] + add[0] + wet * (flow * b_edge[0] - ALPHA_T * dens_grad)
    out[1] = grad_t[1] + add[1] + wet * (flow * b_edge[1] + BETA_S * dens_grad)
    out[2] = grad_u + add[2]
    out[3] = grad_v + add[3]

    arrived(part_copies)
    bg_out[...] = jnp.sum(part_rx[...], axis=0)

    @pl.when(owner)
    def _():
        bg_out[...] = jnp.where(edge, edge_bg[...], bg_out[...])
        for copy in ret2_copies:
            copy.wait_send()

    for to, copy in own_copies:
        pl.when(s != to)(copy.wait_send)
    for copies in (far_copies, early_copies, dens_copies, ret1_copies, part_copies):
        for copy in copies:
            copy.wait_send()


def shards(n_tile, n_store, state, cotangent, land_mask, wet_count, background):
    tile = (8, 128)
    vmem = functools.partial(pltpu.VMEM, dtype=F32)
    sem = pltpu.SemaphoreType.DMA
    n, mates = n_store, n_store - 1
    grad, bg_sum = pl.pallas_call(
        functools.partial(kernel, n_tile, n_store),
        name="ocean",
        out_shape=(jax.ShapeDtypeStruct(state.shape, F32), jax.ShapeDtypeStruct(tile, F32)),
        in_specs=[pl.BlockSpec(memory_space=pl.ANY)] * 5,
        out_specs=(pl.BlockSpec(memory_space=pltpu.VMEM), pl.BlockSpec(memory_space=pltpu.VMEM)),
        scratch_shapes=[
            vmem(state.shape), vmem(state.shape),
            pltpu.VMEM(tile, jnp.int32), pltpu.VMEM(tile, jnp.int32), vmem(tile),
            vmem((2,) + tile), vmem((2,) + tile), vmem((2, 2) + tile), vmem((n, 2) + tile), vmem((n, 2) + tile),
            vmem((2,) + tile), vmem((2,) + tile),
            vmem((n, 3) + tile), vmem((n, 3) + tile),
            vmem((n, 2) + tile), vmem((n, 2) + tile),
            vmem((n,) + tile), vmem((2,) + tile),
            vmem(tile), vmem((n,) + tile), vmem(tile),
            sem((5,)), sem((2,)), sem((2,)), sem((2,)), sem((n,)), sem((2,)), sem((n,)), sem((2,)), sem((2,)),
            sem((mates,)), sem((mates,)), sem((mates,)), sem((mates,)), sem((mates,)), sem((2,)),
            sem((mates,)), sem((mates,)), pltpu.SemaphoreType.REGULAR, pltpu.SemaphoreType.REGULAR,
        ],
        compiler_params=pltpu.CompilerParams(collective_id=0, has_side_effects=True),
    )(state, cotangent, land_mask, wet_count, background)
    part = state.shape[3] // n_store
    return grad, lax.dynamic_slice_in_dim(bg_sum, lax.axis_index("store") * part, part, 1)


def solution(mesh):
    in_specs = (
        P(None, "store", None, "tile"),
        P(None, "store", None, "tile"),
        P(None, "tile"),
        P(None, "tile"),
        P(None, "tile"),
    )
    out_specs = (P(None, "store", None, "tile"), P(None, ("tile", "store")))
    body = functools.partial(shards, mesh.shape["tile"], mesh.shape["store"])
    return jax.shard_map(body, mesh=mesh, in_specs=in_specs, out_specs=out_specs, check_vma=False)
```

```python
import functools

import jax
import jax.numpy as jnp
from jax import lax
from jax.experimental import pallas as pl
from jax.experimental.pallas import tpu as pltpu
from jax.sharding import PartitionSpec as P

DIFFUSE = 0.1
ADVECT = 0.05
MIXING = 2.0
ALPHA_T = 0.6
BETA_S = 0.8
MESH = pl.DeviceIdType.MESH
F32 = jnp.float32


def lanes(x, shift):
    shift %= 128
    return pltpu.roll(x, shift, x.ndim - 1) if shift else x


def rows(x, shift):
    return pltpu.roll(x, shift % 8, x.ndim - 2)


def kernel(
    n_tile, n_store, state_h, cot_h, land_h, count_h, bg_h, out, bg_out,
    st, ct, land, count, bg,
    xa, xb, halo_rx, far_rx, own_rx, dens_tx, dens_rx,
    early, early_rx, ret1, ret1_rx, ret2, ret2_rx, part, part_rx, edge_bg,
    in_sem, halo_s, halo_r, far_s, far_r, own_s, own_r, dens_s, dens_r,
    early_s, early_r, ret1_s, ret1_r, ret2_s, ret2_r, part_s, part_r, near, far,
):
    t = lax.axis_index("tile")
    s = lax.axis_index("store")
    east = lax.rem(t + 1, n_tile)
    west = lax.rem(t + n_tile - 1, n_tile)
    below = lax.rem(s + 1, n_store)
    above = lax.rem(s + n_store - 1, n_store)
    end = n_store - 1
    owner = jnp.logical_or(s == 0, s == end)
    late = lax.rem(t // 4, 2) == 1

    barrier = pltpu.get_barrier_semaphore()

    def greet(**where):
        pl.semaphore_signal(barrier, inc=1, device_id=where, device_id_type=MESH)

    core = lax.rem(s, 2)
    chip = s - core
    other = {"store": chip + 1 - core}
    for to in (east, west):
        greet(tile=to, store=chip + 1)
    greet(**other)
    for d in range(2, n_store, 2):
        greet(store=lax.rem(chip + d, n_store))

    @pl.when(s == 0)
    def _():
        for d in range(1, n_store, 2):
            greet(tile=west, store=d)

    @pl.when(s == end)
    def _():
        for d in range(1, n_store, 2):
            greet(tile=east, store=d)

    loads = [
        pltpu.make_async_copy(src, dst, in_sem.at[i])
        for i, (src, dst) in enumerate(((land_h, land), (count_h, count), (bg_h, bg), (state_h, st), (cot_h, ct)))
    ]
    for load in loads:
        load.start()

    lane = lax.broadcasted_iota(jnp.int32, (8, 128), 1)
    row = lax.broadcasted_iota(jnp.int32, (8, 128), 0)
    block = lane >> 4
    field = (lane & 15) >> 1
    even = (lane & 1) == 0
    pairs = ((lane + 1) & 127) >> 1
    first = lane == 0
    last = lane == 127
    edge = jnp.logical_or(first, last)

    def send(src, dst, send_sem, recv_sem, where):
        return pltpu.make_async_remote_copy(
            src_ref=src, dst_ref=dst, send_sem=send_sem, recv_sem=recv_sem, device_id=where, device_id_type=MESH
        )

    def mates(src, dst, send_sem, recv_sem):
        copies = []
        for d in range(1, n_store):
            to = lax.rem(s + d, n_store)
            copies.append(send(src(to), dst.at[s], send_sem.at[d - 1], recv_sem.at[d - 1], {"store": to}))
        return copies

    def start(copies):
        for copy in copies:
            copy.start()

    def arrived(copies):
        for copy in copies:
            copy.wait_recv()

    def exchange_blocks(tiles):
        tiles = list(tiles)
        for b in (4, 2, 1):
            keep = (block & b) == 0
            new = [None] * 8
            for v in range(8):
                if v & b == 0:
                    lo, hi = tiles[v], tiles[v + b]
                    new[v] = jnp.where(keep, lo, lanes(hi, 16 * b))
                    new[v + b] = jnp.where(keep, lanes(lo, -16 * b), hi)
            tiles = new
        return tiles

    def pack_edges(tiles, bits):
        for bit in bits:
            half = tiles.shape[0] // 2
            tiles = jnp.where((pairs & bit) != 0, lanes(tiles[half:], 2 * bit), tiles[:half])
        return jnp.where(even, tiles[0], lanes(tiles[0], 2))

    def column(x, c):
        return jnp.broadcast_to(x[:, c : c + 1], (8, 128))

    def to_north(x):
        return jnp.where(row == 7, 0.0, rows(x, 7))

    def to_south(x):
        return jnp.where(row == 0, 0.0, rows(x, 1))

    def eliminate(mix):
        ratio, inverse = [], []
        excess = jnp.ones((8, 128), F32)
        for i in range(7):
            inv = 1.0 / (excess + mix[i])
            ratio.append(mix[i] * inv)
            inverse.append(inv)
            excess = 1.0 + ratio[i] * excess
        inverse.append(1.0 / excess)
        up = [inverse[0]]
        for i in range(1, 8):
            up.append(mix[i - 1] * up[-1] * inverse[i])
        for i in range(6, -1, -1):
            up[i] = up[i] + ratio[i] * up[i + 1]
        down = [None] * 7 + [inverse[7]]
        for i in range(6, -1, -1):
            down[i] = ratio[i] * down[i + 1]
        return (mix, ratio, inverse), up, down

    def local_solve(system, rhs):
        mix, ratio, inverse = system
        values = [rhs[0] * inverse[0]]
        for i in range(1, 8):
            values.append((rhs[i] + mix[i - 1] * values[-1]) * inverse[i])
        for i in range(6, -1, -1):
            values[i] = values[i] + ratio[i] * values[i + 1]
        return values

    def edge_system(tiles, start_level, depths, backs):
        dens = -ALPHA_T * tiles + BETA_S * lanes(tiles, -2)
        for bit in (1, 2, 4):
            dens = jnp.where((field & bit) == 0, dens, lanes(dens, 2 * bit))
        wets = jnp.where(jnp.stack([start_level + i for i in range(8)]) < depths, 1.0, 0.0)
        mixes = (backs + MIXING * jax.nn.sigmoid(dens[:-1] - dens[1:])) * wets[1:]
        return dens, wets, eliminate(mixes)

    def reduce_blocks(tiles):
        m_all, m_inv, low, high = [], [], [], []
        for j in range(7):
            here, there = tiles[j], tiles[j + 1]
            weight = lanes(here, -80)
            gates = jax.nn.sigmoid(lanes(here, -64) - lanes(there, -48))
            m = jnp.where(weight > 0.0, weight + MIXING * gates, 0.0)
            pivot = 1.0 + m * (lanes(here, -32) + there)
            lower = m * lanes(here, -16)
            if j:
                pivot = pivot - lower * high[-1]
            inv = 1.0 / jnp.where(block == 0, pivot, 1.0)
            m_all.append(m)
            m_inv.append(m * inv)
            low.append(lower * inv)
            high.append(m * lanes(there, -16) * inv)
        return m_all, m_inv, low, high

    def fluxes(m_inv, low, high, jumps):
        flux = []
        for j in range(7):
            value = m_inv[j] * jumps[j]
            flux.append(value + low[j] * flux[-1] if j else value)
        for j in range(5, -1, -1):
            flux[j] = flux[j] + high[j] * flux[j + 1]
        return flux

    level = (lax.broadcasted_iota(jnp.int32, (8, 8, 128), 0) + s * 8).astype(F32)
    base = (s * 8).astype(F32)

    for load in loads:
        load.wait()
    depth = jnp.where(land[...] == 1, count[...], 0).astype(F32)
    wet = jnp.where(level < depth, 1.0, 0.0)
    backgr = bg[...]
    masked = st[...] * wet
    xa[0] = jnp.where(jnp.logical_or(lane < 32, lane >= 96), depth, lanes(backgr, 64))
    fields = [masked[f] for f in range(4)] + [ct[f] for f in range(4)]
    own_edges = pack_edges(jnp.stack([fields[f][i] for i in range(8) for f in range(8)]), (32, 16, 8, 4, 2, 1))
    xa[1] = own_edges
    xb[0] = own_edges

    far_copies = [
        send(xa, far_rx.at[s], far_s.at[0], far_r.at[s], {"tile": east, "store": 0}),
        send(xa, far_rx.at[s], far_s.at[1], far_r.at[s], {"tile": west, "store": end}),
        send(xa, halo_rx.at[0], halo_s.at[0], halo_r.at[0], {"tile": east}),
        send(xa, halo_rx.at[1], halo_s.at[1], halo_r.at[1], {"tile": west}),
    ]

    def to_neighbours():
        @pl.when(core == 1)
        def _():
            pl.semaphore_wait(barrier, 7)
            pl.semaphore_signal(far, inc=1, device_id=other, device_id_type=MESH)

        @pl.when(core == 0)
        def _():
            pl.semaphore_wait(far, 1)

        start(far_copies)

    pl.when(late)(to_neighbours)

    density = -ALPHA_T * masked[0] + BETA_S * masked[1]
    dens_tx[0] = density[7]
    dens_tx[1] = density[0]
    gate = jax.nn.sigmoid(density[:-1] - density[1:])
    pair = wet[1:]
    system, up, down = eliminate((backgr + MIXING * gate) * pair)
    p_back = local_solve(system, [ct[:, i] for i in range(8)])

    shift_e = jnp.where(last, 0.0, lanes(masked, 127))
    shift_w = jnp.where(first, 0.0, lanes(masked, 1))
    around = jnp.where(level < jnp.where(last, 0.0, lanes(depth, 127)), 1.0, 0.0)
    around += jnp.where(level < jnp.where(first, 0.0, lanes(depth, 1)), 1.0, 0.0)
    around += jnp.where(level < to_north(depth), 1.0, 0.0)
    around += jnp.where(level < to_south(depth), 1.0, 0.0)
    centre = wet * (1.0 - DIFFUSE * around)
    spread = DIFFUSE * wet
    m_north = to_north(masked)
    m_south = to_south(masked)
    latitude = 0.1 + 0.2 * (row.astype(F32) + 0.5) / 8.0
    inter = centre * masked + spread * (shift_e + shift_w + m_north + m_south)
    zonal, merid = masked[2], masked[3]
    grad_x = shift_e[:2] - shift_w[:2]
    grad_y = m_north[:2] - m_south[:2]
    advect = -ADVECT * (zonal * grad_x + merid * grad_y)
    inter = [inter[0] + advect[0], inter[1] + advect[1], inter[2] + latitude * merid, inter[3] - latitude * zonal]
    xb[1] = pack_edges(jnp.stack([inter[f][i] for i in range(8) for f in range(4)]), (32, 16, 8, 2, 1))
    inter = jnp.stack(inter)
    p_after = local_solve(system, [inter[:, i] for i in range(8)])

    bottom_wet = base + 8.0 < depth
    bg_pair = jnp.where(bottom_wet, backgr, 0.0)
    groups = (
        [p_back[0][f] for f in range(4)] + [p_back[7][f] for f in range(4)],
        [p_after[0][f] for f in range(4)] + [p_after[7][f] for f in range(4)],
        [up[0], up[7], down[7], density[0], density[7], bg_pair, bg_pair, bg_pair],
    )
    for g, group in enumerate(groups):
        for d, tile in enumerate(exchange_blocks(group)):
            early[d, g] = tile
    early_rx[s] = early[s]
    own_rx[s] = xb[...]

    @pl.when(core == 0)
    def _():
        pl.semaphore_wait(barrier, end)
        pl.semaphore_signal(near, inc=1, device_id=other, device_id_type=MESH)

    @pl.when(core == 1)
    def _():
        pl.semaphore_wait(near, 1)

    early_copies = mates(lambda to: early.at[to], early_rx, early_s, early_r)
    start(early_copies)
    dens_copies = [
        send(dens_tx.at[0], dens_rx.at[0], dens_s.at[0], dens_r.at[0], {"store": below}),
        send(dens_tx.at[1], dens_rx.at[1], dens_s.at[1], dens_r.at[1], {"store": above}),
    ]
    start(dens_copies)
    own_copies = [
        (to, send(xb, own_rx.at[s], own_s.at[k], own_r.at[s], {"store": to})) for k, to in enumerate((0, end))
    ]
    for to, copy in own_copies:
        pl.when(s != to)(copy.start)

    pl.when(jnp.logical_not(late))(to_neighbours)

    arrived(early_copies)
    _, *coefs = reduce_blocks([early_rx[j, 2] for j in range(8)])

    def four(x):
        x = jnp.where(block == 0, x, lanes(x, 16))
        return jnp.where(block < 2, x, lanes(x, 32))

    coefs = [[four(x) for x in xs] for xs in coefs]
    left = lane < 64
    for g in range(2):
        ends = [early_rx[j, g] for j in range(8)]
        flux = fluxes(*coefs, [lanes(ends[j], 64) - ends[j + 1] for j in range(7)])
        for d in range(8):
            above_flux = flux[d - 1] if d else 0.0
            below_flux = lanes(flux[d], 64) if d < 7 else 0.0
            ret1[d, g] = jnp.where(left, above_flux, below_flux)
    ret1_rx[s] = ret1[s]
    ret1_copies = mates(lambda to: ret1.at[to], ret1_rx, ret1_s, ret1_r)
    start(ret1_copies)

    arrived(dens_copies)
    gate_top = jax.nn.sigmoid(dens_rx[0] - density[0])
    gate_bot = jax.nn.sigmoid(density[7] - dens_rx[1])
    pair_top = jnp.where(base > 0.0, wet[0], 0.0)
    pair_bot = jnp.where(bottom_wet, 1.0, 0.0)
    scale_top = pair_top / (backgr + MIXING * gate_top)
    scale_bot = pair_bot / (backgr + MIXING * gate_bot)

    def coefficients(after, top_a, bot_a):
        coef = -jnp.sum(diff_b * (after[:, :-1] - after[:, 1:]), axis=0) * pair
        coef_top = -jnp.sum(top_b * top_a, axis=0) * (scale_top * scale_top)
        coef_bot = -jnp.sum(bot_b * bot_a, axis=0) * (scale_bot * scale_bot)
        return coef, coef_top, coef_bot

    def finish(p, top, bot):
        return jnp.stack([p[i] + up[i] * top - down[i] * bot for i in range(8)], axis=1)

    arrived(ret1_copies)
    flux_b = exchange_blocks([ret1_rx[d, 0] for d in range(8)])
    flux_a = exchange_blocks([ret1_rx[d, 1] for d in range(8)])
    top_b, bot_b = jnp.stack(flux_b[:4]), jnp.stack(flux_b[4:])
    top_a, bot_a = jnp.stack(flux_a[:4]), jnp.stack(flux_a[4:])
    back = finish(p_back, top_b, bot_b)
    diff_b = back[:, :-1] - back[:, 1:]
    coef, _, coef_bot = coefficients(finish(p_after, top_a, bot_a), top_a, bot_a)
    total = jnp.sum(coef, axis=0) + coef_bot
    part[...] = total
    part_rx[s] = total
    part_copies = mates(lambda to: part, part_rx, part_s, part_r)
    start(part_copies)

    mine = lax.rem(s, 2)
    ret2_copies = [
        send(ret2.at[lax.rem(s + d, n_store)], ret2_rx.at[mine], ret2_s.at[d - 1], ret2_r.at[mine],
             {"store": lax.rem(s + d, n_store)})
        for d in range(1, n_store)
    ]

    @pl.when(owner)
    def _():
        for d in range(1, n_store):
            src = lax.rem(s + d, n_store)
            send(xb, own_rx.at[src], own_s.at[0], own_r.at[src], {"store": src}).wait_recv()
        for src in range(n_store):
            send(xa, far_rx.at[src], far_s.at[0], far_r.at[src], {"tile": east}).wait_recv()
        is_own = (lane & 1) == mine
        own = exchange_blocks([own_rx[j, 0] for j in range(8)])
        inter0 = jnp.stack(exchange_blocks([own_rx[j, 1] for j in range(8)]))
        halo = exchange_blocks([far_rx[j, 1] for j in range(8)])
        both = jnp.stack([jnp.where(is_own, own[i], halo[i]) for i in range(8)])
        there = far_rx[0, 0]

        def sides(x, a, b):
            return jnp.where(even, column(x, a), column(x, b))

        depths = jnp.where(is_own, sides(depth, 0, 127), sides(there, 0, 127))
        backs = jnp.where(is_own, sides(backgr, 0, 127), sides(there, 64, 63))
        start_level = (block * 8).astype(F32)
        dens, wets, (edge_sys, e_up, e_down) = edge_system(both, start_level, depths, backs)

        def swap(x):
            return jnp.where(even, lanes(x, -1), lanes(x, 1))

        m_halo = swap(both)
        along = jnp.where(field == 0, lanes(both, -4), lanes(both, -2)) * jnp.where(even, ADVECT, -ADVECT)
        delta = DIFFUSE * wets * (m_halo - swap(wets) * both) + jnp.where(field < 2, along * m_halo, 0.0)
        rhs = jnp.where(field < 4, jnp.where(is_own, inter0 + delta, 0.0), both)
        p = local_solve(edge_sys, [rhs[i] for i in range(8)])
        weight = jnp.where(start_level + 8.0 < depths, backs, 0.0)
        blocks = exchange_blocks([e_up[0], e_up[7], e_down[7], dens[0], dens[7], weight, p[0], p[7]])
        m_all, *e_coefs = reduce_blocks(blocks)
        flux = fluxes(*e_coefs, [lanes(blocks[j], -112) - lanes(blocks[j + 1], -96) for j in range(7)])
        for d in range(8):
            above_flux = flux[d - 1] if d else 0.0
            below_flux = lanes(flux[d], 16) if d < 7 else 0.0
            ret2[d] = jnp.where(block == 0, above_flux, jnp.where(block == 1, below_flux, 0.0))
        ret2_rx[mine] = ret2[s]
        start(ret2_copies)

        top = jnp.zeros((8, 128), F32)
        bot = jnp.zeros((8, 128), F32)
        for j in range(7):
            top = jnp.where(block == j + 1, lanes(flux[j], 16 * (j + 1)), top)
            bot = jnp.where(block == j, lanes(flux[j], 16 * j), bot)
        x = jnp.stack([p[i] + e_up[i] * top - e_down[i] * bot for i in range(8)])
        diff = x[:-1] - x[1:]
        result = jnp.sum(wets[1:] * diff * lanes(diff, -8), axis=0)
        for shift in (64, 32, 16):
            result = result + lanes(result, shift)
        for j in range(7):
            jump = jnp.where(m_all[j] > 0.0, flux[j] / m_all[j], 0.0)
            result = result + jump * lanes(jump, -8)
        result = result + lanes(result, -2)
        result = -(result + lanes(result, -4))
        edge_bg[...] = jnp.where(first, result, lanes(result, 126))

    wet_back = wet * back
    b_east = jnp.where(last, 0.0, lanes(wet_back, 127))
    b_west = jnp.where(first, 0.0, lanes(wet_back, 1))
    b_north = to_north(wet_back)
    b_south = to_south(wet_back)
    grad = centre * wet_back + spread * (b_east + b_west + b_north + b_south)
    flow = shift_e[2] * b_east[:2] - shift_w[2] * b_west[:2] + m_north[3] * b_north[:2] - m_south[3] * b_south[:2]
    grad_t = grad[:2] + ADVECT * wet * flow
    grad_u = grad[2] - ADVECT * jnp.sum(wet_back[:2] * grad_x, axis=0) - latitude * wet_back[3]
    grad_v = grad[3] - ADVECT * jnp.sum(wet_back[:2] * grad_y, axis=0) + latitude * wet_back[2]

    arrived(far_copies[2:])
    from_west, from_east = halo_rx[0], halo_rx[1]
    cols = jnp.where(even, from_east[1], from_west[1])
    cols = jnp.stack([lanes(cols, -16 * i) for i in range(8)])
    depths = jnp.where(even, column(from_east[0], 0), column(from_west[0], 127))
    backs = jnp.where(even, column(from_east[0], 64), column(from_west[0], 63))
    _, h_wet, (h_sys, h_up, h_down) = edge_system(cols, jnp.full((8, 128), base), depths, backs)
    p_halo = local_solve(h_sys, [cols[i] for i in range(8)])
    m_halo = jnp.stack([lanes(cols, 127 - 2 * f) for f in range(4)])
    depth_halo = jnp.where(last, column(from_east[0], 0), column(from_west[0], 127))
    edge_wet = jnp.where(jnp.logical_and(edge, level < depth_halo), wet, 0.0)
    sign = jnp.where(last, ADVECT, jnp.where(first, -ADVECT, 0.0))
    m_edge = jnp.where(edge, m_halo, 0.0)
    delta = spread * m_edge - DIFFUSE * edge_wet * masked
    delta_t = delta[:2] - sign * zonal * m_edge[:2]
    delta = inter + jnp.concatenate([delta_t, delta[2:]], axis=0)
    p_after = local_solve(system, [delta[:, i] for i in range(8)])
    grad_t = grad_t - DIFFUSE * edge_wet * wet_back[:2]
    grad_u = grad_u - DIFFUSE * edge_wet * wet_back[2] - sign * jnp.sum(wet_back[:2] * m_edge[:2], axis=0)
    grad_v = grad_v - DIFFUSE * edge_wet * wet_back[3]

    arrived(part_copies)
    bg_out[...] = jnp.sum(part_rx[...], axis=0)

    @pl.when(owner)
    def _():
        bg_out[...] = jnp.where(edge, edge_bg[...], bg_out[...])

    for k, to in enumerate((0, end)):

        @pl.when(s != to)
        def _():
            send(ret2.at[0], ret2_rx.at[k], ret2_s.at[0], ret2_r.at[k], {"store": to}).wait_recv()

    west_edge, east_edge = ret2_rx[0], ret2_rx[1]
    own = jnp.where(even, west_edge, lanes(east_edge, -2))
    top_a = jnp.where(edge, jnp.stack([lanes(own, -2 * f) for f in range(4)]), top_a)
    bot_a = jnp.where(edge, jnp.stack([lanes(own, -2 * f - 16) for f in range(4)]), bot_a)
    coef, coef_top, coef_bot = coefficients(finish(p_after, top_a, bot_a), top_a, bot_a)
    slope = MIXING * coef * gate * (1.0 - gate)
    slope_top = MIXING * coef_top * gate_top * (1.0 - gate_top)
    slope_bot = MIXING * coef_bot * gate_bot * (1.0 - gate_bot)
    dens_grad = jnp.concatenate([slope, slope_bot[None]], axis=0) - jnp.concatenate([slope_top[None], slope], axis=0)

    h_flux = jnp.where(even, east_edge, west_edge)
    h_bot = lanes(h_flux, -16)
    h_back = h_wet * jnp.stack([p_halo[i] + h_up[i] * h_flux - h_down[i] * h_bot for i in range(8)])
    b_edge = jnp.where(edge, jnp.stack([lanes(h_back, 119 - 2 * f) for f in range(4)]), 0.0)
    flow = sign * m_edge[2]
    add = spread * b_edge
    out[0] = grad_t[0] + add[0] + wet * (flow * b_edge[0] - ALPHA_T * dens_grad)
    out[1] = grad_t[1] + add[1] + wet * (flow * b_edge[1] + BETA_S * dens_grad)
    out[2] = grad_u + add[2]
    out[3] = grad_v + add[3]

    @pl.when(owner)
    def _():
        for copy in ret2_copies:
            copy.wait_send()

    for to, copy in own_copies:
        pl.when(s != to)(copy.wait_send)
    for copies in (far_copies, early_copies, dens_copies, ret1_copies, part_copies):
        for copy in copies:
            copy.wait_send()


def shards(n_tile, n_store, state, cotangent, land_mask, wet_count, background):
    tile = (8, 128)
    vmem = functools.partial(pltpu.VMEM, dtype=F32)
    sem = pltpu.SemaphoreType.DMA
    n, mates = n_store, n_store - 1
    grad, bg_sum = pl.pallas_call(
        functools.partial(kernel, n_tile, n_store),
        name="ocean",
        out_shape=(jax.ShapeDtypeStruct(state.shape, F32), jax.ShapeDtypeStruct(tile, F32)),
        in_specs=[pl.BlockSpec(memory_space=pltpu.HBM)] * 5,
        out_specs=(pl.BlockSpec(memory_space=pltpu.VMEM), pl.BlockSpec(memory_space=pltpu.VMEM)),
        scratch_shapes=[
            vmem(state.shape), vmem(state.shape),
            pltpu.VMEM(tile, jnp.int32), pltpu.VMEM(tile, jnp.int32), vmem(tile),
            vmem((2,) + tile), vmem((2,) + tile), vmem((2, 2) + tile), vmem((n, 2) + tile), vmem((n, 2) + tile),
            vmem((2,) + tile), vmem((2,) + tile),
            vmem((n, 3) + tile), vmem((n, 3) + tile),
            vmem((n, 2) + tile), vmem((n, 2) + tile),
            vmem((n,) + tile), vmem((2,) + tile),
            vmem(tile), vmem((n,) + tile), vmem(tile),
            sem((5,)), sem((2,)), sem((2,)), sem((2,)), sem((n,)), sem((2,)), sem((n,)), sem((2,)), sem((2,)),
            sem((mates,)), sem((mates,)), sem((mates,)), sem((mates,)), sem((mates,)), sem((2,)),
            sem((mates,)), sem((mates,)), pltpu.SemaphoreType.REGULAR, pltpu.SemaphoreType.REGULAR,
        ],
        compiler_params=pltpu.CompilerParams(collective_id=0, has_side_effects=True, vmem_limit_bytes=8 << 20),
    )(*[pltpu.with_memory_space_constraint(x, pltpu.HBM) for x in (state, cotangent, land_mask, wet_count, background)])
    part = state.shape[3] // n_store
    return grad, lax.dynamic_slice_in_dim(bg_sum, lax.axis_index("store") * part, part, 1)


def solution(mesh):
    in_specs = (
        P(None, "store", None, "tile"),
        P(None, "store", None, "tile"),
        P(None, "tile"),
        P(None, "tile"),
        P(None, "tile"),
    )
    out_specs = (P(None, "store", None, "tile"), P(None, ("tile", "store")))
    body = functools.partial(shards, mesh.shape["tile"], mesh.shape["store"])
    return jax.shard_map(body, mesh=mesh, in_specs=in_specs, out_specs=out_specs, check_vma=False)
```

```python
import functools

import jax
import jax.numpy as jnp
from jax import lax
from jax.experimental import pallas as pl
from jax.experimental.pallas import tpu as pltpu
from jax.sharding import PartitionSpec as P

DIFFUSE = 0.1
ADVECT = 0.05
MIXING = 2.0
ALPHA_T = 0.6
BETA_S = 0.8
MESH = pl.DeviceIdType.MESH
F32 = jnp.float32


def lanes(x, shift):
    shift %= 128
    return pltpu.roll(x, shift, x.ndim - 1) if shift else x


def rows(x, shift):
    return pltpu.roll(x, shift % 8, x.ndim - 2)


def kernel(
    n_tile, n_store, state_h, cot_h, land_h, count_h, bg_h, out, bg_out,
    st, ct, land, count, bg,
    xa, xb, halo_rx, own_rx, dens_tx, dens_rx,
    early, early_rx, ret1, ret1_rx, part, part_rx, back_tx, back_rx,
    in_sem, halo_s, halo_r, own_s, own_r, dens_s, dens_r,
    early_s, early_r, ret1_s, ret1_r, part_s, part_r, back_s, back_r, near, far,
):
    t = lax.axis_index("tile")
    s = lax.axis_index("store")
    east = lax.rem(t + 1, n_tile)
    west = lax.rem(t + n_tile - 1, n_tile)
    below = lax.rem(s + 1, n_store)
    above = lax.rem(s + n_store - 1, n_store)
    end = n_store - 1
    owner = jnp.logical_or(s == 0, s == end)
    late = lax.rem(t // 4, 2) == 1

    barrier = pltpu.get_barrier_semaphore()

    def greet(**where):
        pl.semaphore_signal(barrier, inc=1, device_id=where, device_id_type=MESH)

    core = lax.rem(s, 2)
    chip = s - core
    other = {"store": chip + 1 - core}
    for to in (east, west):
        for d in range(1, n_store, 2):
            greet(tile=to, store=d)
    greet(**other)
    for d in range(2, n_store, 2):
        greet(store=lax.rem(chip + d, n_store))

    loads = [
        pltpu.make_async_copy(src, dst, in_sem.at[i])
        for i, (src, dst) in enumerate(((land_h, land), (count_h, count), (bg_h, bg), (state_h, st), (cot_h, ct)))
    ]
    for load in loads:
        load.start()

    lane = lax.broadcasted_iota(jnp.int32, (8, 128), 1)
    row = lax.broadcasted_iota(jnp.int32, (8, 128), 0)
    block = lane >> 4
    field = (lane & 15) >> 1
    even = (lane & 1) == 0
    pairs = ((lane + 1) & 127) >> 1
    first = lane == 0
    last = lane == 127
    edge = jnp.logical_or(first, last)

    def send(src, dst, send_sem, recv_sem, where):
        return pltpu.make_async_remote_copy(
            src_ref=src, dst_ref=dst, send_sem=send_sem, recv_sem=recv_sem, device_id=where, device_id_type=MESH
        )

    def mates(src, dst, send_sem, recv_sem):
        copies = []
        for d in range(1, n_store):
            to = lax.rem(s + d, n_store)
            copies.append(send(src(to), dst.at[s], send_sem.at[d - 1], recv_sem.at[d - 1], {"store": to}))
        return copies

    def start(copies):
        for copy in copies:
            copy.start()

    def arrived(copies):
        for copy in copies:
            copy.wait_recv()

    def exchange_blocks(tiles):
        tiles = list(tiles)
        for b in (4, 2, 1):
            keep = (block & b) == 0
            new = [None] * 8
            for v in range(8):
                if v & b == 0:
                    lo, hi = tiles[v], tiles[v + b]
                    new[v] = jnp.where(keep, lo, lanes(hi, 16 * b))
                    new[v + b] = jnp.where(keep, lanes(lo, -16 * b), hi)
            tiles = new
        return tiles

    def pack_edges(tiles, bits):
        for bit in bits:
            half = tiles.shape[0] // 2
            tiles = jnp.where((pairs & bit) != 0, lanes(tiles[half:], 2 * bit), tiles[:half])
        return tiles[0]

    def beside(x):
        return jnp.where(even, x, lanes(x, 2))

    def column(x, c):
        return jnp.broadcast_to(x[:, c : c + 1], (8, 128))

    def to_north(x):
        return jnp.where(row == 7, 0.0, rows(x, 7))

    def to_south(x):
        return jnp.where(row == 0, 0.0, rows(x, 1))

    def eliminate(mix):
        ratio, inverse = [], []
        excess = jnp.ones((8, 128), F32)
        for i in range(7):
            inv = 1.0 / (excess + mix[i])
            ratio.append(mix[i] * inv)
            inverse.append(inv)
            excess = 1.0 + ratio[i] * excess
        inverse.append(1.0 / excess)
        up = [inverse[0]]
        for i in range(1, 8):
            up.append(mix[i - 1] * up[-1] * inverse[i])
        for i in range(6, -1, -1):
            up[i] = up[i] + ratio[i] * up[i + 1]
        down = [None] * 7 + [inverse[7]]
        for i in range(6, -1, -1):
            down[i] = ratio[i] * down[i + 1]
        return (mix, ratio, inverse), up, down

    def local_solve(system, rhs):
        mix, ratio, inverse = system
        values = [rhs[0] * inverse[0]]
        for i in range(1, 8):
            values.append((rhs[i] + mix[i - 1] * values[-1]) * inverse[i])
        for i in range(6, -1, -1):
            values[i] = values[i] + ratio[i] * values[i + 1]
        return values

    def edge_density(tiles):
        dens = -ALPHA_T * tiles + BETA_S * lanes(tiles, -2)
        for bit in (1, 2, 4):
            dens = jnp.where((field & bit) == 0, dens, lanes(dens, 2 * bit))
        return dens

    def sides(a, b):
        return jnp.where(even, a, b)

    def reduce_blocks(tiles):
        m_inv, low, high = [], [], []
        for j in range(7):
            here, there = tiles[j], tiles[j + 1]
            weight = lanes(here, -80)
            gates = jax.nn.sigmoid(lanes(here, -64) - lanes(there, -48))
            m = jnp.where(weight > 0.0, weight + MIXING * gates, 0.0)
            pivot = 1.0 + m * (lanes(here, -32) + there)
            lower = m * lanes(here, -16)
            if j:
                pivot = pivot - lower * high[-1]
            inv = 1.0 / jnp.where(block == 0, pivot, 1.0)
            m_inv.append(m * inv)
            low.append(lower * inv)
            high.append(m * lanes(there, -16) * inv)
        return m_inv, low, high

    def fluxes(m_inv, low, high, jumps):
        flux = []
        for j in range(7):
            value = m_inv[j] * jumps[j]
            flux.append(value + low[j] * flux[-1] if j else value)
        for j in range(5, -1, -1):
            flux[j] = flux[j] + high[j] * flux[j + 1]
        return flux

    level = (lax.broadcasted_iota(jnp.int32, (8, 8, 128), 0) + s * 8).astype(F32)
    base = (s * 8).astype(F32)

    for load in loads:
        load.wait()
    depth = jnp.where(land[...] == 1, count[...], 0).astype(F32)
    wet = jnp.where(level < depth, 1.0, 0.0)
    backgr = bg[...]
    masked = st[...] * wet
    fields = [masked[f] for f in range(4)] + [ct[f] for f in range(4)]
    packed = pack_edges(jnp.stack([fields[f][i] for i in range(8) for f in range(8)]), (32, 16, 8, 4, 2, 1))
    own_edges = beside(packed)

    def extra(c):
        return jnp.where(field == 0, column(depth, c), column(backgr, c))

    xa[0] = sides(extra(127), own_edges)
    xa[1] = sides(own_edges, extra(0))
    xb[0] = own_edges
    far_copies = []
    for side, to in enumerate((east, west)):
        for d in range(n_store):
            far_copies.append(
                send(xa.at[side], halo_rx.at[side, s], halo_s.at[side, d], halo_r.at[side, s], {"tile": to, "store": d})
            )

    def to_neighbours():
        @pl.when(core == 1)
        def _():
            pl.semaphore_wait(barrier, 2 * n_store + 1)
            pl.semaphore_signal(far, inc=1, device_id=other, device_id_type=MESH)

        @pl.when(core == 0)
        def _():
            pl.semaphore_wait(far, 1)

        start(far_copies)

    pl.when(late)(to_neighbours)

    density = -ALPHA_T * masked[0] + BETA_S * masked[1]
    dens_tx[0] = density[7]
    dens_tx[1] = density[0]
    gate = jax.nn.sigmoid(density[:-1] - density[1:])
    pair = wet[1:]
    system, up, down = eliminate((backgr + MIXING * gate) * pair)
    p_back = local_solve(system, [ct[:, i] for i in range(8)])

    shift_e = jnp.where(last, 0.0, lanes(masked, 127))
    shift_w = jnp.where(first, 0.0, lanes(masked, 1))
    around = jnp.where(level < jnp.where(last, 0.0, lanes(depth, 127)), 1.0, 0.0)
    around += jnp.where(level < jnp.where(first, 0.0, lanes(depth, 1)), 1.0, 0.0)
    around += jnp.where(level < to_north(depth), 1.0, 0.0)
    around += jnp.where(level < to_south(depth), 1.0, 0.0)
    centre = wet * (1.0 - DIFFUSE * around)
    spread = DIFFUSE * wet
    m_north = to_north(masked)
    m_south = to_south(masked)
    latitude = 0.1 + 0.2 * (row.astype(F32) + 0.5) / 8.0
    inter = centre * masked + spread * (shift_e + shift_w + m_north + m_south)
    zonal, merid = masked[2], masked[3]
    grad_x = shift_e[:2] - shift_w[:2]
    grad_y = m_north[:2] - m_south[:2]
    advect = -ADVECT * (zonal * grad_x + merid * grad_y)
    inter = [inter[0] + advect[0], inter[1] + advect[1], inter[2] + latitude * merid, inter[3] - latitude * zonal]
    xb[1] = beside(pack_edges(jnp.stack([inter[f][i] for i in range(8) for f in range(4)]), (32, 16, 8, 2, 1)))
    inter = jnp.stack(inter)
    p_after = local_solve(system, [inter[:, i] for i in range(8)])

    bottom_wet = base + 8.0 < depth
    bg_pair = jnp.where(bottom_wet, backgr, 0.0)
    groups = (
        [p_back[0][f] for f in range(4)] + [p_back[7][f] for f in range(4)],
        [p_after[0][f] for f in range(4)] + [p_after[7][f] for f in range(4)],
        [up[0], up[7], down[7], density[0], density[7], bg_pair, bg_pair, bg_pair],
    )
    for g, group in enumerate(groups):
        for d, tile in enumerate(exchange_blocks(group)):
            early[d, g] = tile
    early_rx[s] = early[s]
    own_rx[s] = xb[...]

    @pl.when(core == 0)
    def _():
        pl.semaphore_wait(barrier, end)
        pl.semaphore_signal(near, inc=1, device_id=other, device_id_type=MESH)

    @pl.when(core == 1)
    def _():
        pl.semaphore_wait(near, 1)

    early_copies = mates(lambda to: early.at[to], early_rx, early_s, early_r)
    start(early_copies)
    dens_copies = [
        send(dens_tx.at[0], dens_rx.at[0], dens_s.at[0], dens_r.at[0], {"store": below}),
        send(dens_tx.at[1], dens_rx.at[1], dens_s.at[1], dens_r.at[1], {"store": above}),
    ]
    start(dens_copies)
    own_copies = mates(lambda to: xb, own_rx, own_s, own_r)
    start(own_copies)

    arrived(early_copies)
    coefs = reduce_blocks([early_rx[j, 2] for j in range(8)])

    def four(x):
        x = jnp.where(block == 0, x, lanes(x, 16))
        return jnp.where(block < 2, x, lanes(x, 32))

    coefs = [[four(x) for x in xs] for xs in coefs]
    left = lane < 64
    for g in range(2):
        ends = [early_rx[j, g] for j in range(8)]
        flux = fluxes(*coefs, [lanes(ends[j], 64) - ends[j + 1] for j in range(7)])
        for d in range(8):
            above_flux = flux[d - 1] if d else 0.0
            below_flux = lanes(flux[d], 64) if d < 7 else 0.0
            ret1[d, g] = jnp.where(left, above_flux, below_flux)
    ret1_rx[s] = ret1[s]
    ret1_copies = mates(lambda to: ret1.at[to], ret1_rx, ret1_s, ret1_r)
    start(ret1_copies)
    pl.when(jnp.logical_not(late))(to_neighbours)

    arrived(dens_copies)
    gate_top = jax.nn.sigmoid(dens_rx[0] - density[0])
    gate_bot = jax.nn.sigmoid(density[7] - dens_rx[1])
    pair_top = jnp.where(base > 0.0, wet[0], 0.0)
    pair_bot = jnp.where(bottom_wet, 1.0, 0.0)
    scale_top = pair_top / (backgr + MIXING * gate_top)
    scale_bot = pair_bot / (backgr + MIXING * gate_bot)

    def coefficients(after, top_a, bot_a):
        coef = -jnp.sum(diff_b * (after[:, :-1] - after[:, 1:]), axis=0) * pair
        coef_top = -jnp.sum(top_b * top_a, axis=0) * (scale_top * scale_top)
        coef_bot = -jnp.sum(bot_b * bot_a, axis=0) * (scale_bot * scale_bot)
        return coef, coef_top, coef_bot

    def finish(p, top, bot):
        return jnp.stack([p[i] + up[i] * top - down[i] * bot for i in range(8)], axis=1)

    arrived(ret1_copies)
    flux_b = exchange_blocks([ret1_rx[d, 0] for d in range(8)])
    flux_a = exchange_blocks([ret1_rx[d, 1] for d in range(8)])
    top_b, bot_b = jnp.stack(flux_b[:4]), jnp.stack(flux_b[4:])
    top_a, bot_a = jnp.stack(flux_a[:4]), jnp.stack(flux_a[4:])
    back = finish(p_back, top_b, bot_b)
    diff_b = back[:, :-1] - back[:, 1:]
    after = finish(p_after, top_a, bot_a)
    coef, _, coef_bot = coefficients(after, top_a, bot_a)
    total = jnp.sum(coef, axis=0) + coef_bot
    part[...] = total
    part_rx[s] = total
    part_copies = mates(lambda to: part, part_rx, part_s, part_r)
    start(part_copies)
    wet_back = wet * back
    back_tx[...] = beside(pack_edges(jnp.stack([back[f, i] for i in range(8) for f in range(4)]), (32, 16, 8, 2, 1)))
    back_rx[s] = back_tx[...]
    back_copies = [
        (to, send(back_tx, back_rx.at[s], back_s.at[k], back_r.at[s], {"store": to})) for k, to in enumerate((0, end))
    ]
    for to, copy in back_copies:
        pl.when(s != to)(copy.start)


    b_east = jnp.where(last, 0.0, lanes(wet_back, 127))
    b_west = jnp.where(first, 0.0, lanes(wet_back, 1))
    b_north = to_north(wet_back)
    b_south = to_south(wet_back)
    grad = centre * wet_back + spread * (b_east + b_west + b_north + b_south)
    flow = shift_e[2] * b_east[:2] - shift_w[2] * b_west[:2] + m_north[3] * b_north[:2] - m_south[3] * b_south[:2]
    grad_t = grad[:2] + ADVECT * wet * flow
    grad_u = grad[2] - ADVECT * jnp.sum(wet_back[:2] * grad_x, axis=0) - latitude * wet_back[3]
    grad_v = grad[3] - ADVECT * jnp.sum(wet_back[:2] * grad_y, axis=0) + latitude * wet_back[2]

    arrived(own_copies)
    own = jnp.stack(exchange_blocks([own_rx[j, 0] for j in range(8)]))
    own_inter = jnp.stack(exchange_blocks([own_rx[j, 1] for j in range(8)]))
    own_dens = edge_density(own)
    start_level = (block * 8).astype(F32)
    edge_level = jnp.stack([start_level + i for i in range(8)])
    own_depth = sides(column(depth, 0), column(depth, 127))
    own_bg = sides(column(backgr, 0), column(backgr, 127))
    along = jnp.where(field == 0, lanes(own, -4), lanes(own, -2)) * sides(ADVECT, -ADVECT)
    along = jnp.where(field < 2, along, 0.0)
    own_wet = jnp.where(edge_level < own_depth, DIFFUSE, 0.0)

    for side in range(2):
        for src in range(n_store):
            send(xa.at[0], halo_rx.at[side, src], halo_s.at[0, 0], halo_r.at[side, src], {"tile": east}).wait_recv()
    halo = jnp.stack(exchange_blocks([sides(halo_rx[1, j], halo_rx[0, j]) for j in range(8)]))
    from_west, from_east = halo_rx[0, 0], halo_rx[1, 0]
    west_depth, east_depth = column(from_west, 0), column(from_east, 1)
    inner = field < 4
    dens = jnp.where(inner, own_dens, edge_density(halo))
    depths = jnp.where(inner, own_depth, sides(east_depth, west_depth))
    backs = jnp.where(inner, own_bg, sides(column(from_east, 3), column(from_west, 2)))
    edge_wet = jnp.where(edge_level < depths, 1.0, 0.0)
    halo_wet = jnp.where(edge_level < sides(west_depth, east_depth), 1.0, 0.0)
    swapped = sides(lanes(halo, -1), lanes(halo, 1))
    delta = own_wet * (swapped - halo_wet * own) + along * swapped
    rhs = jnp.where(inner, own_inter + delta, halo)
    edge_sys, e_up, e_down = eliminate((backs + MIXING * jax.nn.sigmoid(dens[:-1] - dens[1:])) * edge_wet[1:])
    p = local_solve(edge_sys, [rhs[i] for i in range(8)])
    weight = jnp.where(start_level + 8.0 < depths, backs, 0.0)
    blocks = exchange_blocks([e_up[0], e_up[7], e_down[7], dens[0], dens[7], weight, p[0], p[7]])
    jumps = [lanes(blocks[j], -112) - lanes(blocks[j + 1], -96) for j in range(7)]
    flux = fluxes(*reduce_blocks(blocks), jumps)
    bot = jnp.where(block == 0, flux[0], 0.0)
    for j in range(1, 7):
        bot = jnp.where(block == j, lanes(flux[j], 16 * j), bot)
    top = lanes(bot, 16)
    solved = jnp.stack([p[i] + e_up[i] * top - e_down[i] * bot for i in range(8)])

    here = jnp.concatenate([solved, top[None], bot[None]], axis=0)
    for bit in (1, 2, 4):
        here = jnp.where((s & bit) != 0, lanes(here, -16 * bit), here)
    own_here = sides(here, lanes(here, -2))
    own_here = jnp.stack([lanes(own_here, -2 * f) for f in range(4)])
    after = jnp.where(edge, own_here[:, :8], after)
    top_a = jnp.where(edge, own_here[:, 8], top_a)
    bot_a = jnp.where(edge, own_here[:, 9], bot_a)
    b_edge = jnp.stack([lanes(here[:8], 119 - 2 * f) for f in range(4)])
    cols = sides(halo_rx[1, s], halo_rx[0, s])
    cols = jnp.stack([lanes(cols, -16 * i) for i in range(8)])
    m_edge = jnp.stack([lanes(cols, 127 - 2 * f) for f in range(3)])
    beside_wet = jnp.where(jnp.logical_and(edge, level < jnp.where(last, east_depth, west_depth)), DIFFUSE * wet, 0.0)
    edge_flow = jnp.where(edge, b_edge * beside_wet, 0.0) - beside_wet * wet_back
    sign = jnp.where(last, ADVECT, jnp.where(first, -ADVECT, 0.0))
    flow = jnp.where(edge, sign * m_edge[2] * jnp.where(beside_wet > 0.0, 1.0, 0.0), 0.0)
    coef, coef_top, coef_bot = coefficients(after, top_a, bot_a)
    slope = MIXING * coef * gate * (1.0 - gate)
    slope_top = MIXING * coef_top * gate_top * (1.0 - gate_top)
    slope_bot = MIXING * coef_bot * gate_bot * (1.0 - gate_bot)
    dens_grad = wet * (
        jnp.concatenate([slope, slope_bot[None]], axis=0) - jnp.concatenate([slope_top[None], slope], axis=0)
    )
    pull = jnp.where(edge, sign * jnp.sum(wet_back[:2] * m_edge[:2], axis=0), 0.0)
    out[0] = grad_t[0] + edge_flow[0] + flow * b_edge[0] - ALPHA_T * dens_grad
    out[1] = grad_t[1] + edge_flow[1] + flow * b_edge[1] + BETA_S * dens_grad
    out[2] = grad_u + edge_flow[2] - pull
    out[3] = grad_v + edge_flow[3]

    arrived(part_copies)
    bg_out[...] = jnp.sum(part_rx[...], axis=0)

    @pl.when(owner)
    def _():
        for d in range(1, n_store):
            src = lax.rem(s + d, n_store)
            send(back_tx, back_rx.at[src], back_s.at[0], back_r.at[src], {"store": src}).wait_recv()
        own_back = jnp.stack(exchange_blocks([back_rx[j] for j in range(8)]))
        result = jnp.sum(edge_wet[1:] * (solved[:-1] - solved[1:]) * (own_back[:-1] - own_back[1:]), axis=0)
        jump = (solved[7] - lanes(solved[0], -16)) * (own_back[7] - lanes(own_back[0], -16))
        result = result + jnp.where(weight > 0.0, jump, 0.0)
        for shift in (64, 32, 16):
            result = result + lanes(result, shift)
        result = result + lanes(result, -2)
        result = -(result + lanes(result, -4))
        bg_out[...] = jnp.where(first, result, jnp.where(last, lanes(result, 126), bg_out[...]))

    for to, copy in back_copies:
        pl.when(s != to)(copy.wait_send)
    for copies in (far_copies, early_copies, dens_copies, own_copies, ret1_copies, part_copies):
        for copy in copies:
            copy.wait_send()


def shards(n_tile, n_store, state, cotangent, land_mask, wet_count, background):
    tile = (8, 128)
    vmem = functools.partial(pltpu.VMEM, dtype=F32)
    sem = pltpu.SemaphoreType.DMA
    n, mates = n_store, n_store - 1
    grad, bg_sum = pl.pallas_call(
        functools.partial(kernel, n_tile, n_store),
        name="ocean",
        out_shape=(jax.ShapeDtypeStruct(state.shape, F32), jax.ShapeDtypeStruct(tile, F32)),
        in_specs=[pl.BlockSpec(memory_space=pltpu.HBM)] * 5,
        out_specs=(pl.BlockSpec(memory_space=pltpu.VMEM), pl.BlockSpec(memory_space=pltpu.VMEM)),
        scratch_shapes=[
            vmem(state.shape), vmem(state.shape),
            pltpu.VMEM(tile, jnp.int32), pltpu.VMEM(tile, jnp.int32), vmem(tile),
            vmem((2,) + tile), vmem((2,) + tile), vmem((2, n) + tile), vmem((n, 2) + tile),
            vmem((2,) + tile), vmem((2,) + tile),
            vmem((n, 3) + tile), vmem((n, 3) + tile),
            vmem((n, 2) + tile), vmem((n, 2) + tile),
            vmem(tile), vmem((n,) + tile), vmem(tile), vmem((n,) + tile),
            sem((5,)), sem((2, n)), sem((2, n)), sem((mates,)), sem((mates,)), sem((2,)), sem((2,)),
            sem((mates,)), sem((mates,)), sem((mates,)), sem((mates,)), sem((mates,)), sem((mates,)),
            sem((2,)), sem((n,)), pltpu.SemaphoreType.REGULAR, pltpu.SemaphoreType.REGULAR,
        ],
        compiler_params=pltpu.CompilerParams(collective_id=0, has_side_effects=True, vmem_limit_bytes=8 << 20),
    )(*[pltpu.with_memory_space_constraint(x, pltpu.HBM) for x in (state, cotangent, land_mask, wet_count, background)])
    part = state.shape[3] // n_store
    return grad, lax.dynamic_slice_in_dim(bg_sum, lax.axis_index("store") * part, part, 1)


def solution(mesh):
    in_specs = (
        P(None, "store", None, "tile"),
        P(None, "store", None, "tile"),
        P(None, "tile"),
        P(None, "tile"),
        P(None, "tile"),
    )
    out_specs = (P(None, "store", None, "tile"), P(None, ("tile", "store")))
    body = functools.partial(shards, mesh.shape["tile"], mesh.shape["store"])
    return jax.shard_map(body, mesh=mesh, in_specs=in_specs, out_specs=out_specs, check_vma=False)
```

```python
import functools

import jax
import jax.numpy as jnp
from jax import lax
from jax.experimental import pallas as pl
from jax.experimental.pallas import tpu as pltpu
from jax.sharding import PartitionSpec as P

DIFFUSE = 0.1
ADVECT = 0.05
MIXING = 2.0
ALPHA_T = 0.6
BETA_S = 0.8
MESH = pl.DeviceIdType.MESH
F32 = jnp.float32


def lanes(x, shift):
    shift %= 128
    return pltpu.roll(x, shift, x.ndim - 1) if shift else x


def rows(x, shift):
    return pltpu.roll(x, shift % 8, x.ndim - 2)


def kernel(
    n_tile, n_store, state_h, cot_h, land_h, count_h, bg_h, out, bg_out,
    fields_in, cells_in, bg,
    xa, xb, halo_rx, own_rx, dens_tx, dens_rx,
    early, early_rx, ret1, ret1_rx, part, part_rx, back_tx, back_rx,
    in_sem, halo_s, halo_r, own_s, own_r, dens_s, dens_r,
    early_s, early_r, ret1_s, ret1_r, part_s, part_r, back_s, back_r, near, far,
):
    t = lax.axis_index("tile")
    s = lax.axis_index("store")
    east = lax.rem(t + 1, n_tile)
    west = lax.rem(t + n_tile - 1, n_tile)
    below = lax.rem(s + 1, n_store)
    above = lax.rem(s + n_store - 1, n_store)
    end = n_store - 1
    owner = jnp.logical_or(s == 0, s == end)
    late = lax.rem(t // 4, 2) == 1

    pltpu.make_async_copy(state_h, fields_in.at[0], in_sem.at[0]).start()
    pltpu.make_async_copy(cot_h, fields_in.at[1], in_sem.at[0]).start()
    pltpu.make_async_copy(land_h, cells_in.at[0], in_sem.at[1]).start()
    pltpu.make_async_copy(count_h, cells_in.at[1], in_sem.at[1]).start()
    pltpu.make_async_copy(bg_h, bg, in_sem.at[2]).start()
    st, ct = fields_in.at[0], fields_in.at[1]

    barrier = pltpu.get_barrier_semaphore()

    def greet(**where):
        pl.semaphore_signal(barrier, inc=1, device_id=where, device_id_type=MESH)

    core = lax.rem(s, 2)
    chip = s - core
    other = {"store": chip + 1 - core}
    for to in (east, west):
        for d in range(1, n_store, 2):
            greet(tile=to, store=d)
    greet(**other)
    for d in range(2, n_store, 2):
        greet(store=lax.rem(chip + d, n_store))

    lane = lax.broadcasted_iota(jnp.int32, (8, 128), 1)
    row = lax.broadcasted_iota(jnp.int32, (8, 128), 0)
    block = lane >> 4
    field = (lane & 15) >> 1
    even = (lane & 1) == 0
    pairs = ((lane + 1) & 127) >> 1
    first = lane == 0
    last = lane == 127
    edge = jnp.logical_or(first, last)

    def send(src, dst, send_sem, recv_sem, where):
        return pltpu.make_async_remote_copy(
            src_ref=src, dst_ref=dst, send_sem=send_sem, recv_sem=recv_sem, device_id=where, device_id_type=MESH
        )

    def mates(src, dst, send_sem, recv_sem):
        copies = []
        for d in range(1, n_store):
            to = lax.rem(s + d, n_store)
            copies.append(send(src(to), dst.at[s], send_sem, recv_sem, {"store": to}))
        return copies

    def arrived(ref, sem):
        send(ref, ref, sem, sem, {"tile": east}).wait_recv()

    def sent(ref, sem):
        send(ref, ref, sem, sem, {"tile": east}).wait_send()

    def others(ref):
        return ref.at[pl.ds(0, n_store - 1)]

    def start(copies):
        for copy in copies:
            copy.start()

    def exchange_blocks(tiles):
        tiles = list(tiles)
        for b in (4, 2, 1):
            keep = (block & b) == 0
            new = [None] * 8
            for v in range(8):
                if v & b == 0:
                    lo, hi = tiles[v], tiles[v + b]
                    new[v] = jnp.where(keep, lo, lanes(hi, 16 * b))
                    new[v + b] = jnp.where(keep, lanes(lo, -16 * b), hi)
            tiles = new
        return tiles

    def pack_edges(tiles, bits):
        for bit in bits:
            half = tiles.shape[0] // 2
            tiles = jnp.where((pairs & bit) != 0, lanes(tiles[half:], 2 * bit), tiles[:half])
        return tiles[0]

    def beside(x):
        return jnp.where(even, x, lanes(x, 2))

    def column(x, c):
        return jnp.broadcast_to(x[:, c : c + 1], (8, 128))

    def to_north(x):
        return jnp.where(row == 7, 0.0, rows(x, 7))

    def to_south(x):
        return jnp.where(row == 0, 0.0, rows(x, 1))

    def eliminate(mix):
        ratio, inverse = [], []
        excess = jnp.ones((8, 128), F32)
        for i in range(7):
            inv = 1.0 / (excess + mix[i])
            ratio.append(mix[i] * inv)
            inverse.append(inv)
            excess = 1.0 + ratio[i] * excess
        inverse.append(1.0 / excess)
        up = [inverse[0]]
        for i in range(1, 8):
            up.append(mix[i - 1] * up[-1] * inverse[i])
        for i in range(6, -1, -1):
            up[i] = up[i] + ratio[i] * up[i + 1]
        down = [None] * 7 + [inverse[7]]
        for i in range(6, -1, -1):
            down[i] = ratio[i] * down[i + 1]
        return (mix, ratio, inverse), up, down

    def local_solve(system, rhs):
        mix, ratio, inverse = system
        values = [rhs[0] * inverse[0]]
        for i in range(1, 8):
            values.append((rhs[i] + mix[i - 1] * values[-1]) * inverse[i])
        for i in range(6, -1, -1):
            values[i] = values[i] + ratio[i] * values[i + 1]
        return values

    def edge_density(tiles):
        dens = -ALPHA_T * tiles + BETA_S * lanes(tiles, -2)
        for bit in (1, 2, 4):
            dens = jnp.where((field & bit) == 0, dens, lanes(dens, 2 * bit))
        return dens

    def sides(a, b):
        return jnp.where(even, a, b)

    def reduce_blocks(tiles):
        m_inv, low, high = [], [], []
        for j in range(7):
            here, there = tiles[j], tiles[j + 1]
            weight = lanes(here, -80)
            gates = jax.nn.sigmoid(lanes(here, -64) - lanes(there, -48))
            m = jnp.where(weight > 0.0, weight + MIXING * gates, 0.0)
            pivot = 1.0 + m * (lanes(here, -32) + there)
            lower = m * lanes(here, -16)
            if j:
                pivot = pivot - lower * high[-1]
            inv = 1.0 / jnp.where(block == 0, pivot, 1.0)
            m_inv.append(m * inv)
            low.append(lower * inv)
            high.append(m * lanes(there, -16) * inv)
        return m_inv, low, high

    def fluxes(m_inv, low, high, jumps):
        flux = []
        for j in range(7):
            value = m_inv[j] * jumps[j]
            flux.append(value + low[j] * flux[-1] if j else value)
        for j in range(5, -1, -1):
            flux[j] = flux[j] + high[j] * flux[j + 1]
        return flux

    level = (lax.broadcasted_iota(jnp.int32, (8, 8, 128), 0) + s * 8).astype(F32)
    base = (s * 8).astype(F32)

    pltpu.make_async_copy(cells_in, cells_in, in_sem.at[1]).wait()
    pltpu.make_async_copy(bg, bg, in_sem.at[2]).wait()
    pltpu.make_async_copy(fields_in, fields_in, in_sem.at[0]).wait()
    depth = jnp.where(cells_in[0] == 1, cells_in[1], 0).astype(F32)
    wet = jnp.where(level < depth, 1.0, 0.0)
    backgr = bg[...]
    masked = st[...] * wet
    fields = [masked[f] for f in range(4)] + [ct[f] for f in range(4)]
    packed = pack_edges(jnp.stack([fields[f][i] for i in range(8) for f in range(8)]), (32, 16, 8, 4, 2, 1))
    own_edges = beside(packed)

    def extra(c):
        return jnp.where(field == 0, column(depth, c), column(backgr, c))

    xa[0] = sides(extra(127), own_edges)
    xa[1] = sides(own_edges, extra(0))
    xb[0] = own_edges
    far_copies = []
    for side, to in enumerate((east, west)):
        for d in range(n_store):
            far_copies.append(
                send(xa.at[side], halo_rx.at[side, s], halo_s, halo_r, {"tile": to, "store": d})
            )

    def to_neighbours():
        @pl.when(core == 1)
        def _():
            pl.semaphore_wait(barrier, 2 * n_store + 1)
            pl.semaphore_signal(far, inc=1, device_id=other, device_id_type=MESH)

        @pl.when(core == 0)
        def _():
            pl.semaphore_wait(far, 1)

        start(far_copies)

    pl.when(late)(to_neighbours)

    density = -ALPHA_T * masked[0] + BETA_S * masked[1]
    dens_tx[0] = density[7]
    dens_tx[1] = density[0]
    gate = jax.nn.sigmoid(density[:-1] - density[1:])
    pair = wet[1:]
    system, up, down = eliminate((backgr + MIXING * gate) * pair)
    p_back = local_solve(system, [ct[:, i] for i in range(8)])

    shift_e = jnp.where(last, 0.0, lanes(masked, 127))
    shift_w = jnp.where(first, 0.0, lanes(masked, 1))
    around = jnp.where(level < jnp.where(last, 0.0, lanes(depth, 127)), 1.0, 0.0)
    around += jnp.where(level < jnp.where(first, 0.0, lanes(depth, 1)), 1.0, 0.0)
    around += jnp.where(level < to_north(depth), 1.0, 0.0)
    around += jnp.where(level < to_south(depth), 1.0, 0.0)
    centre = wet * (1.0 - DIFFUSE * around)
    spread = DIFFUSE * wet
    m_north = to_north(masked)
    m_south = to_south(masked)
    latitude = 0.1 + 0.2 * (row.astype(F32) + 0.5) / 8.0
    inter = centre * masked + spread * (shift_e + shift_w + m_north + m_south)
    zonal, merid = masked[2], masked[3]
    grad_x = shift_e[:2] - shift_w[:2]
    grad_y = m_north[:2] - m_south[:2]
    advect = -ADVECT * (zonal * grad_x + merid * grad_y)
    inter = [inter[0] + advect[0], inter[1] + advect[1], inter[2] + latitude * merid, inter[3] - latitude * zonal]
    xb[1] = beside(pack_edges(jnp.stack([inter[f][i] for i in range(8) for f in range(4)]), (32, 16, 8, 2, 1)))
    inter = jnp.stack(inter)
    p_after = local_solve(system, [inter[:, i] for i in range(8)])

    bottom_wet = base + 8.0 < depth
    bg_pair = jnp.where(bottom_wet, backgr, 0.0)
    groups = (
        [p_back[0][f] for f in range(4)] + [p_back[7][f] for f in range(4)],
        [p_after[0][f] for f in range(4)] + [p_after[7][f] for f in range(4)],
        [up[0], up[7], down[7], density[0], density[7], bg_pair, bg_pair, bg_pair],
    )
    for g, group in enumerate(groups):
        for d, tile in enumerate(exchange_blocks(group)):
            early[d, g] = tile
    early_rx[s] = early[s]
    own_rx[s] = xb[...]

    @pl.when(core == 0)
    def _():
        pl.semaphore_wait(barrier, end)
        pl.semaphore_signal(near, inc=1, device_id=other, device_id_type=MESH)

    @pl.when(core == 1)
    def _():
        pl.semaphore_wait(near, 1)

    early_copies = mates(lambda to: early.at[to], early_rx, early_s, early_r)
    start(early_copies)
    dens_copies = [
        send(dens_tx.at[0], dens_rx.at[0], dens_s, dens_r, {"store": below}),
        send(dens_tx.at[1], dens_rx.at[1], dens_s, dens_r, {"store": above}),
    ]
    start(dens_copies)
    own_copies = mates(lambda to: xb, own_rx, own_s, own_r)
    start(own_copies)

    arrived(others(early_rx), early_r)
    coefs = reduce_blocks([early_rx[j, 2] for j in range(8)])

    def four(x):
        x = jnp.where(block == 0, x, lanes(x, 16))
        return jnp.where(block < 2, x, lanes(x, 32))

    coefs = [[four(x) for x in xs] for xs in coefs]
    left = lane < 64
    for g in range(2):
        ends = [early_rx[j, g] for j in range(8)]
        flux = fluxes(*coefs, [lanes(ends[j], 64) - ends[j + 1] for j in range(7)])
        for d in range(8):
            above_flux = flux[d - 1] if d else 0.0
            below_flux = lanes(flux[d], 64) if d < 7 else 0.0
            ret1[d, g] = jnp.where(left, above_flux, below_flux)
    ret1_rx[s] = ret1[s]
    ret1_copies = mates(lambda to: ret1.at[to], ret1_rx, ret1_s, ret1_r)
    start(ret1_copies)
    pl.when(jnp.logical_not(late))(to_neighbours)

    arrived(dens_rx, dens_r)
    gate_top = jax.nn.sigmoid(dens_rx[0] - density[0])
    gate_bot = jax.nn.sigmoid(density[7] - dens_rx[1])
    pair_top = jnp.where(base > 0.0, wet[0], 0.0)
    pair_bot = jnp.where(bottom_wet, 1.0, 0.0)
    scale_top = pair_top / (backgr + MIXING * gate_top)
    scale_bot = pair_bot / (backgr + MIXING * gate_bot)

    def coefficients(after, top_a, bot_a):
        coef = -jnp.sum(diff_b * (after[:, :-1] - after[:, 1:]), axis=0) * pair
        coef_top = -jnp.sum(top_b * top_a, axis=0) * (scale_top * scale_top)
        coef_bot = -jnp.sum(bot_b * bot_a, axis=0) * (scale_bot * scale_bot)
        return coef, coef_top, coef_bot

    def finish(p, top, bot):
        return jnp.stack([p[i] + up[i] * top - down[i] * bot for i in range(8)], axis=1)

    arrived(others(ret1_rx), ret1_r)
    flux_b = exchange_blocks([ret1_rx[d, 0] for d in range(8)])
    flux_a = exchange_blocks([ret1_rx[d, 1] for d in range(8)])
    top_b, bot_b = jnp.stack(flux_b[:4]), jnp.stack(flux_b[4:])
    top_a, bot_a = jnp.stack(flux_a[:4]), jnp.stack(flux_a[4:])
    back = finish(p_back, top_b, bot_b)
    diff_b = back[:, :-1] - back[:, 1:]
    after = finish(p_after, top_a, bot_a)
    coef, _, coef_bot = coefficients(after, top_a, bot_a)
    total = jnp.sum(coef, axis=0) + coef_bot
    part[...] = total
    part_rx[s] = total
    part_copies = mates(lambda to: part, part_rx, part_s, part_r)
    start(part_copies)
    wet_back = wet * back
    back_tx[...] = beside(pack_edges(jnp.stack([back[f, i] for i in range(8) for f in range(4)]), (32, 16, 8, 2, 1)))
    back_rx[s] = back_tx[...]
    back_copies = [
        (to, send(back_tx, back_rx.at[s], back_s, back_r, {"store": to})) for to in (0, end)
    ]
    for to, copy in back_copies:
        pl.when(s != to)(copy.start)


    b_east = jnp.where(last, 0.0, lanes(wet_back, 127))
    b_west = jnp.where(first, 0.0, lanes(wet_back, 1))
    b_north = to_north(wet_back)
    b_south = to_south(wet_back)
    grad = centre * wet_back + spread * (b_east + b_west + b_north + b_south)
    flow = shift_e[2] * b_east[:2] - shift_w[2] * b_west[:2] + m_north[3] * b_north[:2] - m_south[3] * b_south[:2]
    grad_t = grad[:2] + ADVECT * wet * flow
    grad_u = grad[2] - ADVECT * jnp.sum(wet_back[:2] * grad_x, axis=0) - latitude * wet_back[3]
    grad_v = grad[3] - ADVECT * jnp.sum(wet_back[:2] * grad_y, axis=0) + latitude * wet_back[2]

    arrived(others(own_rx), own_r)
    own = jnp.stack(exchange_blocks([own_rx[j, 0] for j in range(8)]))
    own_inter = jnp.stack(exchange_blocks([own_rx[j, 1] for j in range(8)]))
    own_dens = edge_density(own)
    start_level = (block * 8).astype(F32)
    edge_level = jnp.stack([start_level + i for i in range(8)])
    own_depth = sides(column(depth, 0), column(depth, 127))
    own_bg = sides(column(backgr, 0), column(backgr, 127))
    along = jnp.where(field == 0, lanes(own, -4), lanes(own, -2)) * sides(ADVECT, -ADVECT)
    along = jnp.where(field < 2, along, 0.0)
    own_wet = jnp.where(edge_level < own_depth, DIFFUSE, 0.0)

    arrived(halo_rx, halo_r)
    halo = jnp.stack(exchange_blocks([sides(halo_rx[1, j], halo_rx[0, j]) for j in range(8)]))
    from_west, from_east = halo_rx[0, 0], halo_rx[1, 0]
    west_depth, east_depth = column(from_west, 0), column(from_east, 1)
    inner = field < 4
    dens = jnp.where(inner, own_dens, edge_density(halo))
    depths = jnp.where(inner, own_depth, sides(east_depth, west_depth))
    backs = jnp.where(inner, own_bg, sides(column(from_east, 3), column(from_west, 2)))
    edge_wet = jnp.where(edge_level < depths, 1.0, 0.0)
    halo_wet = jnp.where(edge_level < sides(west_depth, east_depth), 1.0, 0.0)
    swapped = sides(lanes(halo, -1), lanes(halo, 1))
    delta = own_wet * (swapped - halo_wet * own) + along * swapped
    rhs = jnp.where(inner, own_inter + delta, halo)
    edge_sys, e_up, e_down = eliminate((backs + MIXING * jax.nn.sigmoid(dens[:-1] - dens[1:])) * edge_wet[1:])
    p = local_solve(edge_sys, [rhs[i] for i in range(8)])
    weight = jnp.where(start_level + 8.0 < depths, backs, 0.0)
    blocks = exchange_blocks([e_up[0], e_up[7], e_down[7], dens[0], dens[7], weight, p[0], p[7]])
    jumps = [lanes(blocks[j], -112) - lanes(blocks[j + 1], -96) for j in range(7)]
    flux = fluxes(*reduce_blocks(blocks), jumps)
    bot = jnp.where(block == 0, flux[0], 0.0)
    for j in range(1, 7):
        bot = jnp.where(block == j, lanes(flux[j], 16 * j), bot)
    top = lanes(bot, 16)
    solved = jnp.stack([p[i] + e_up[i] * top - e_down[i] * bot for i in range(8)])

    here = jnp.concatenate([solved, top[None], bot[None]], axis=0)
    for bit in (1, 2, 4):
        here = jnp.where((s & bit) != 0, lanes(here, -16 * bit), here)
    own_here = sides(here, lanes(here, -2))
    own_here = jnp.stack([lanes(own_here, -2 * f) for f in range(4)])
    after = jnp.where(edge, own_here[:, :8], after)
    top_a = jnp.where(edge, own_here[:, 8], top_a)
    bot_a = jnp.where(edge, own_here[:, 9], bot_a)
    b_edge = jnp.stack([lanes(here[:8], 119 - 2 * f) for f in range(4)])
    cols = sides(halo_rx[1, s], halo_rx[0, s])
    cols = jnp.stack([lanes(cols, -16 * i) for i in range(8)])
    m_edge = jnp.stack([lanes(cols, 127 - 2 * f) for f in range(3)])
    beside_wet = jnp.where(jnp.logical_and(edge, level < jnp.where(last, east_depth, west_depth)), DIFFUSE * wet, 0.0)
    edge_flow = jnp.where(edge, b_edge * beside_wet, 0.0) - beside_wet * wet_back
    sign = jnp.where(last, ADVECT, jnp.where(first, -ADVECT, 0.0))
    flow = jnp.where(edge, sign * m_edge[2] * jnp.where(beside_wet > 0.0, 1.0, 0.0), 0.0)
    coef, coef_top, coef_bot = coefficients(after, top_a, bot_a)
    slope = MIXING * coef * gate * (1.0 - gate)
    slope_top = MIXING * coef_top * gate_top * (1.0 - gate_top)
    slope_bot = MIXING * coef_bot * gate_bot * (1.0 - gate_bot)
    dens_grad = wet * (
        jnp.concatenate([slope, slope_bot[None]], axis=0) - jnp.concatenate([slope_top[None], slope], axis=0)
    )
    pull = jnp.where(edge, sign * jnp.sum(wet_back[:2] * m_edge[:2], axis=0), 0.0)
    out[0] = grad_t[0] + edge_flow[0] + flow * b_edge[0] - ALPHA_T * dens_grad
    out[1] = grad_t[1] + edge_flow[1] + flow * b_edge[1] + BETA_S * dens_grad
    out[2] = grad_u + edge_flow[2] - pull
    out[3] = grad_v + edge_flow[3]

    arrived(others(part_rx), part_r)
    bg_out[...] = jnp.sum(part_rx[...], axis=0)

    @pl.when(owner)
    def _():
        arrived(others(back_rx), back_r)
        own_back = jnp.stack(exchange_blocks([back_rx[j] for j in range(8)]))
        result = jnp.sum(edge_wet[1:] * (solved[:-1] - solved[1:]) * (own_back[:-1] - own_back[1:]), axis=0)
        jump = (solved[7] - lanes(solved[0], -16)) * (own_back[7] - lanes(own_back[0], -16))
        result = result + jnp.where(weight > 0.0, jump, 0.0)
        for shift in (64, 32, 16):
            result = result + lanes(result, shift)
        result = result + lanes(result, -2)
        result = -(result + lanes(result, -4))
        bg_out[...] = jnp.where(first, result, jnp.where(last, lanes(result, 126), bg_out[...]))

        sent(back_rx.at[0], back_s)

    @pl.when(jnp.logical_not(owner))
    def _():
        sent(back_rx.at[pl.ds(0, 2)], back_s)

    sent(halo_rx, halo_s)
    sent(dens_rx, dens_s)
    sent(others(early_rx), early_s)
    sent(others(own_rx), own_s)
    sent(others(ret1_rx), ret1_s)
    sent(others(part_rx), part_s)


def shards(n_tile, n_store, state, cotangent, land_mask, wet_count, background):
    tile = (8, 128)
    vmem = functools.partial(pltpu.VMEM, dtype=F32)
    sem = pltpu.SemaphoreType.DMA
    n = n_store
    grad, bg_sum = pl.pallas_call(
        functools.partial(kernel, n_tile, n_store),
        name="ocean",
        out_shape=(jax.ShapeDtypeStruct(state.shape, F32), jax.ShapeDtypeStruct(tile, F32)),
        in_specs=[pl.BlockSpec(memory_space=pltpu.HBM)] * 5,
        out_specs=(pl.BlockSpec(memory_space=pltpu.VMEM), pl.BlockSpec(memory_space=pltpu.VMEM)),
        scratch_shapes=[
            vmem((2,) + state.shape), pltpu.VMEM((2,) + tile, jnp.int32), vmem(tile),
            vmem((2,) + tile), vmem((2,) + tile), vmem((2, n) + tile), vmem((n, 2) + tile),
            vmem((2,) + tile), vmem((2,) + tile),
            vmem((n, 3) + tile), vmem((n, 3) + tile),
            vmem((n, 2) + tile), vmem((n, 2) + tile),
            vmem(tile), vmem((n,) + tile), vmem(tile), vmem((n,) + tile),
            sem((3,)),
        ] + [sem] * 14 + [pltpu.SemaphoreType.REGULAR] * 2,
        compiler_params=pltpu.CompilerParams(collective_id=0, has_side_effects=True, vmem_limit_bytes=8 << 20),
    )(*[pltpu.with_memory_space_constraint(x, pltpu.HBM) for x in (state, cotangent, land_mask, wet_count, background)])
    part = state.shape[3] // n_store
    return grad, lax.dynamic_slice_in_dim(bg_sum, lax.axis_index("store") * part, part, 1)


def solution(mesh):
    in_specs = (
        P(None, "store", None, "tile"),
        P(None, "store", None, "tile"),
        P(None, "tile"),
        P(None, "tile"),
        P(None, "tile"),
    )
    out_specs = (P(None, "store", None, "tile"), P(None, ("tile", "store")))
    body = functools.partial(shards, mesh.shape["tile"], mesh.shape["store"])
    return jax.shard_map(body, mesh=mesh, in_specs=in_specs, out_specs=out_specs, check_vma=False)
```

```python
import functools

import jax
import jax.numpy as jnp
from jax import lax
from jax.experimental import pallas as pl
from jax.experimental.pallas import tpu as pltpu
from jax.sharding import PartitionSpec as P

DIFFUSE = 0.1
ADVECT = 0.05
MIXING = 2.0
ALPHA_T = 0.6
BETA_S = 0.8
MESH = pl.DeviceIdType.MESH
F32 = jnp.float32


def lanes(x, shift):
    shift %= 128
    return pltpu.roll(x, shift, x.ndim - 1) if shift else x


def rows(x, shift):
    return pltpu.roll(x, shift % 8, x.ndim - 2)


def kernel(
    n_tile, n_store, state_h, cot_h, land_h, count_h, bg_h, out, bg_out,
    fields_in, cells_in, bg,
    xa, ya, xb, halo_rx, side_rx, own_rx, dens_tx, dens_rx,
    early, early_rx, ret1, ret1_rx, part, part_rx, back_tx, back_rx,
    in_sem, halo_s, halo_r, side_s, side_r, own_s, own_r, dens_s, dens_r,
    early_s, early_r, ret1_s, ret1_r, part_s, part_r, back_s, back_r, near, far,
):
    t = lax.axis_index("tile")
    s = lax.axis_index("store")
    east = lax.rem(t + 1, n_tile)
    west = lax.rem(t + n_tile - 1, n_tile)
    below = lax.rem(s + 1, n_store)
    above = lax.rem(s + n_store - 1, n_store)
    end = n_store - 1
    owner = jnp.logical_or(s == 0, s == end)
    late = lax.rem(t // 4, 2) == 1

    pltpu.make_async_copy(state_h, fields_in.at[0], in_sem.at[0]).start()
    pltpu.make_async_copy(cot_h, fields_in.at[1], in_sem.at[0]).start()
    pltpu.make_async_copy(land_h, cells_in.at[0], in_sem.at[1]).start()
    pltpu.make_async_copy(count_h, cells_in.at[1], in_sem.at[1]).start()
    pltpu.make_async_copy(bg_h, bg, in_sem.at[2]).start()
    st, ct = fields_in.at[0], fields_in.at[1]

    barrier = pltpu.get_barrier_semaphore()

    def greet(**where):
        pl.semaphore_signal(barrier, inc=1, device_id=where, device_id_type=MESH)

    core = lax.rem(s, 2)
    chip = s - core
    other = {"store": chip + 1 - core}
    for to in (east, west):
        for d in range(1, n_store, 2):
            greet(tile=to, store=d)
    greet(**other)
    for d in range(2, n_store, 2):
        greet(store=lax.rem(chip + d, n_store))

    lane = lax.broadcasted_iota(jnp.int32, (8, 128), 1)
    row = lax.broadcasted_iota(jnp.int32, (8, 128), 0)
    block = lane >> 4
    field = (lane & 15) >> 1
    even = (lane & 1) == 0
    pairs = ((lane + 1) & 127) >> 1
    first = lane == 0
    last = lane == 127
    edge = jnp.logical_or(first, last)

    def send(src, dst, send_sem, recv_sem, where):
        return pltpu.make_async_remote_copy(
            src_ref=src, dst_ref=dst, send_sem=send_sem, recv_sem=recv_sem, device_id=where, device_id_type=MESH
        )

    def mates(src, dst, send_sem, recv_sem):
        copies = []
        for d in range(1, n_store):
            to = lax.rem(s + d, n_store)
            copies.append(send(src(to), dst.at[s], send_sem, recv_sem, {"store": to}))
        return copies

    def arrived(ref, sem):
        send(ref, ref, sem, sem, {"tile": east}).wait_recv()

    def sent(ref, sem):
        send(ref, ref, sem, sem, {"tile": east}).wait_send()

    def others(ref):
        return ref.at[pl.ds(0, n_store - 1)]

    def start(copies):
        for copy in copies:
            copy.start()

    def exchange_blocks(tiles):
        tiles = list(tiles)
        for b in (4, 2, 1):
            keep = (block & b) == 0
            new = [None] * 8
            for v in range(8):
                if v & b == 0:
                    lo, hi = tiles[v], tiles[v + b]
                    new[v] = jnp.where(keep, lo, lanes(hi, 16 * b))
                    new[v + b] = jnp.where(keep, lanes(lo, -16 * b), hi)
            tiles = new
        return tiles

    def pack_edges(tiles, bits):
        for bit in bits:
            half = tiles.shape[0] // 2
            tiles = jnp.where((pairs & bit) != 0, lanes(tiles[half:], 2 * bit), tiles[:half])
        return tiles[0]

    def beside(x):
        return jnp.where(even, x, lanes(x, 2))

    def column(x, c):
        return jnp.broadcast_to(x[:, c : c + 1], (8, 128))

    def to_north(x):
        return jnp.where(row == 7, 0.0, rows(x, 7))

    def to_south(x):
        return jnp.where(row == 0, 0.0, rows(x, 1))

    def eliminate(mix):
        ratio, inverse = [None] * 8, [None] * 8
        above_excess = jnp.ones((8, 128), F32)
        below_excess = jnp.ones((8, 128), F32)
        for i in range(4):
            inverse[i] = 1.0 / (above_excess + mix[i])
            ratio[i] = mix[i] * inverse[i]
            above_excess = 1.0 + ratio[i] * above_excess
        for i in (7, 6, 5):
            inverse[i] = 1.0 / (below_excess + mix[i - 1])
            ratio[i] = mix[i - 1] * inverse[i]
            below_excess = 1.0 + ratio[i] * below_excess
        inverse[4] = 1.0 / (above_excess + (below_excess - 1.0))
        up, down = [None] * 8, [None] * 8
        up[0] = inverse[0]
        for i in range(1, 5):
            up[i] = mix[i - 1] * up[i - 1] * inverse[i]
        for i in (3, 2, 1, 0):
            up[i] = up[i] + ratio[i] * up[i + 1]
        for i in (5, 6, 7):
            up[i] = ratio[i] * up[i - 1]
        down[7] = inverse[7]
        for i in (6, 5, 4):
            down[i] = mix[i] * down[i + 1] * inverse[i]
        for i in (3, 2, 1, 0):
            down[i] = ratio[i] * down[i + 1]
        for i in (5, 6, 7):
            down[i] = down[i] + ratio[i] * down[i - 1]
        return (mix, ratio, inverse), up, down

    def local_solve(system, rhs):
        mix, ratio, inverse = system
        values = [None] * 8
        values[0] = rhs[0] * inverse[0]
        for i in range(1, 4):
            values[i] = (rhs[i] + mix[i - 1] * values[i - 1]) * inverse[i]
        values[7] = rhs[7] * inverse[7]
        for i in (6, 5):
            values[i] = (rhs[i] + mix[i] * values[i + 1]) * inverse[i]
        values[4] = (rhs[4] + mix[3] * values[3] + mix[4] * values[5]) * inverse[4]
        for i in (3, 2, 1, 0):
            values[i] = values[i] + ratio[i] * values[i + 1]
        for i in (5, 6, 7):
            values[i] = values[i] + ratio[i] * values[i - 1]
        return values

    def edge_density(tiles):
        dens = -ALPHA_T * tiles + BETA_S * lanes(tiles, -2)
        for bit in (1, 2, 4):
            dens = jnp.where((field & bit) == 0, dens, lanes(dens, 2 * bit))
        return dens

    def sides(a, b):
        return jnp.where(even, a, b)

    def reduce_blocks(tiles):
        rows_m, diag, lower, upper = [], [], [], []
        for j in range(7):
            here, there = tiles[j], tiles[j + 1]
            weight = lanes(here, -80)
            gates = jax.nn.sigmoid(lanes(here, -64) - lanes(there, -48))
            m = jnp.where(weight > 0.0, weight + MIXING * gates, 0.0)
            rows_m.append(m)
            diag.append(1.0 + m * (lanes(here, -32) + there))
            lower.append(m * lanes(here, -16))
            upper.append(m * lanes(there, -16))
        inv = [None] * 7

        def invert(j, pivot):
            inv[j] = 1.0 / jnp.where(block == 0, pivot, 1.0)

        invert(0, diag[0])
        invert(6, diag[6])
        for j, k in ((1, 5), (2, 4)):
            invert(j, diag[j] - lower[j] * (upper[j - 1] * inv[j - 1]))
            invert(k, diag[k] - upper[k] * (lower[k + 1] * inv[k + 1]))
        invert(3, diag[3] - lower[3] * (upper[2] * inv[2]) - upper[3] * (lower[4] * inv[4]))
        return tuple([x[j] * inv[j] for j in range(7)] for x in (rows_m, lower, upper))

    def fluxes(m_inv, low, high, jumps):
        flux = [m_inv[j] * jumps[j] for j in range(7)]
        for j, k in ((1, 5), (2, 4)):
            flux[j] = flux[j] + low[j] * flux[j - 1]
            flux[k] = flux[k] + high[k] * flux[k + 1]
        flux[3] = flux[3] + low[3] * flux[2] + high[3] * flux[4]
        for j, k in ((2, 4), (1, 5), (0, 6)):
            flux[j] = flux[j] + high[j] * flux[j + 1]
            flux[k] = flux[k] + low[k] * flux[k - 1]
        return flux

    level = (lax.broadcasted_iota(jnp.int32, (8, 8, 128), 0) + s * 8).astype(F32)
    base = (s * 8).astype(F32)

    pltpu.make_async_copy(cells_in, cells_in, in_sem.at[1]).wait()
    pltpu.make_async_copy(bg, bg, in_sem.at[2]).wait()
    pltpu.make_async_copy(fields_in, fields_in, in_sem.at[0]).wait()
    depth = jnp.where(cells_in[0] == 1, cells_in[1], 0).astype(F32)
    wet = jnp.where(level < depth, 1.0, 0.0)
    backgr = bg[...]
    masked = st[...] * wet
    fields = [masked[f] for f in range(4)] + [ct[f] for f in range(4)]
    def store_edges():
        packed = pack_edges(jnp.stack([fields[f][i] for i in range(8) for f in range(8)]), (32, 16, 8, 4, 2, 1))
        own_edges = beside(packed)

        turned = rows(own_edges, 4)
        xa[0] = sides(lanes(own_edges, -1), turned)
        xa[1] = sides(own_edges, lanes(turned, 1))
        ya[...] = jnp.where(jnp.logical_or(lane < 32, lane >= 96), depth, lanes(backgr, 64))
        xb[0] = own_edges
    pl.when(late)(store_edges)

    far_copies = []
    for side, to in enumerate((east, west)):
        for d in range(n_store):
            half = pl.ds(4 - 4 * side, 4)
            far_copies.append(
                send(xa.at[side, pl.ds(0, 4)], halo_rx.at[s, half], halo_s, halo_r, {"tile": to, "store": d})
            )
    far_copies.append(send(ya, side_rx.at[0], side_s, side_r, {"tile": east}))
    far_copies.append(send(ya, side_rx.at[1], side_s, side_r, {"tile": west}))

    def to_neighbours():
        @pl.when(core == 1)
        def _():
            pl.semaphore_wait(barrier, 2 * n_store + 1)
            pl.semaphore_signal(far, inc=1, device_id=other, device_id_type=MESH)

        @pl.when(core == 0)
        def _():
            pl.semaphore_wait(far, 1)

        start(far_copies)

    pl.when(late)(to_neighbours)

    density = -ALPHA_T * masked[0] + BETA_S * masked[1]
    dens_tx[0] = density[7]
    dens_tx[1] = density[0]
    gate = jax.nn.sigmoid(density[:-1] - density[1:])
    pair = wet[1:]
    system, up, down = eliminate((backgr + MIXING * gate) * pair)
    p_back = local_solve(system, [ct[:, i] for i in range(8)])

    shift_e = jnp.where(last, 0.0, lanes(masked, 127))
    shift_w = jnp.where(first, 0.0, lanes(masked, 1))
    around = jnp.where(level < jnp.where(last, 0.0, lanes(depth, 127)), 1.0, 0.0)
    around += jnp.where(level < jnp.where(first, 0.0, lanes(depth, 1)), 1.0, 0.0)
    around += jnp.where(level < to_north(depth), 1.0, 0.0)
    around += jnp.where(level < to_south(depth), 1.0, 0.0)
    centre = wet * (1.0 - DIFFUSE * around)
    spread = DIFFUSE * wet
    m_north = to_north(masked)
    m_south = to_south(masked)
    latitude = 0.1 + 0.2 * (row.astype(F32) + 0.5) / 8.0
    inter = centre * masked + spread * (shift_e + shift_w + m_north + m_south)
    zonal, merid = masked[2], masked[3]
    grad_x = shift_e[:2] - shift_w[:2]
    grad_y = m_north[:2] - m_south[:2]
    advect = -ADVECT * (zonal * grad_x + merid * grad_y)
    inter = [inter[0] + advect[0], inter[1] + advect[1], inter[2] + latitude * merid, inter[3] - latitude * zonal]
    inter_edges = [inter[f][i] for i in range(8) for f in range(4)]
    inter = jnp.stack(inter)
    p_after = local_solve(system, [inter[:, i] for i in range(8)])

    bottom_wet = base + 8.0 < depth
    bg_pair = jnp.where(bottom_wet, backgr, 0.0)
    groups = (
        [p_back[0][f] for f in range(4)] + [p_back[7][f] for f in range(4)],
        [p_after[0][f] for f in range(4)] + [p_after[7][f] for f in range(4)],
        [up[0], up[7], down[7], density[0], density[7], bg_pair, bg_pair, bg_pair],
    )
    for g, group in enumerate(groups):
        for d, tile in enumerate(exchange_blocks(group)):
            early[d, g] = tile
    early_rx[s] = early[s]

    @pl.when(core == 0)
    def _():
        pl.semaphore_wait(barrier, end)
        pl.semaphore_signal(near, inc=1, device_id=other, device_id_type=MESH)

    @pl.when(core == 1)
    def _():
        pl.semaphore_wait(near, 1)

    early_copies = mates(lambda to: early.at[to], early_rx, early_s, early_r)
    start(early_copies)
    dens_copies = [
        send(dens_tx.at[0], dens_rx.at[0], dens_s, dens_r, {"store": below}),
        send(dens_tx.at[1], dens_rx.at[1], dens_s, dens_r, {"store": above}),
    ]
    start(dens_copies)
    pl.when(jnp.logical_not(late))(store_edges)
    xb[1] = beside(pack_edges(jnp.stack(inter_edges), (32, 16, 8, 2, 1)))
    own_rx[s] = xb[...]
    own_copies = mates(lambda to: xb, own_rx, own_s, own_r)
    start(own_copies)

    arrived(others(early_rx), early_r)
    coefs = reduce_blocks([early_rx[j, 2] for j in range(8)])

    def four(x):
        x = jnp.where(block == 0, x, lanes(x, 16))
        return jnp.where(block < 2, x, lanes(x, 32))

    coefs = [[four(x) for x in xs] for xs in coefs]
    left = lane < 64
    for g in range(2):
        ends = [early_rx[j, g] for j in range(8)]
        flux = fluxes(*coefs, [lanes(ends[j], 64) - ends[j + 1] for j in range(7)])
        for d in range(8):
            above_flux = flux[d - 1] if d else 0.0
            below_flux = lanes(flux[d], 64) if d < 7 else 0.0
            ret1[d, g] = jnp.where(left, above_flux, below_flux)
    ret1_rx[s] = ret1[s]
    ret1_copies = mates(lambda to: ret1.at[to], ret1_rx, ret1_s, ret1_r)
    start(ret1_copies)
    pl.when(jnp.logical_not(late))(to_neighbours)

    arrived(dens_rx, dens_r)
    gate_top = jax.nn.sigmoid(dens_rx[0] - density[0])
    gate_bot = jax.nn.sigmoid(density[7] - dens_rx[1])
    pair_top = jnp.where(base > 0.0, wet[0], 0.0)
    pair_bot = jnp.where(bottom_wet, 1.0, 0.0)
    scale_top = pair_top / (backgr + MIXING * gate_top)
    scale_bot = pair_bot / (backgr + MIXING * gate_bot)

    def coefficients(after, top_a, bot_a):
        coef = -jnp.sum(diff_b * (after[:, :-1] - after[:, 1:]), axis=0) * pair
        coef_top = -jnp.sum(top_b * top_a, axis=0) * (scale_top * scale_top)
        coef_bot = -jnp.sum(bot_b * bot_a, axis=0) * (scale_bot * scale_bot)
        return coef, coef_top, coef_bot

    def finish(p, top, bot):
        return jnp.stack([p[i] + up[i] * top - down[i] * bot for i in range(8)], axis=1)

    arrived(others(ret1_rx), ret1_r)
    flux_b = exchange_blocks([ret1_rx[d, 0] for d in range(8)])
    flux_a = exchange_blocks([ret1_rx[d, 1] for d in range(8)])
    top_b, bot_b = jnp.stack(flux_b[:4]), jnp.stack(flux_b[4:])
    top_a, bot_a = jnp.stack(flux_a[:4]), jnp.stack(flux_a[4:])
    back = finish(p_back, top_b, bot_b)
    diff_b = back[:, :-1] - back[:, 1:]
    after = finish(p_after, top_a, bot_a)
    coef, _, coef_bot = coefficients(after, top_a, bot_a)
    total = jnp.sum(coef, axis=0) + coef_bot
    part[...] = total
    part_rx[s] = total
    part_copies = mates(lambda to: part, part_rx, part_s, part_r)
    start(part_copies)
    wet_back = wet * back
    back_tx[...] = beside(pack_edges(jnp.stack([back[f, i] for i in range(8) for f in range(4)]), (32, 16, 8, 2, 1)))
    back_rx[s] = back_tx[...]
    back_copies = [
        (to, send(back_tx, back_rx.at[s], back_s, back_r, {"store": to})) for to in (0, end)
    ]
    for to, copy in back_copies:
        pl.when(s != to)(copy.start)


    b_east = jnp.where(last, 0.0, lanes(wet_back, 127))
    b_west = jnp.where(first, 0.0, lanes(wet_back, 1))
    b_north = to_north(wet_back)
    b_south = to_south(wet_back)
    grad = centre * wet_back + spread * (b_east + b_west + b_north + b_south)
    flow = shift_e[2] * b_east[:2] - shift_w[2] * b_west[:2] + m_north[3] * b_north[:2] - m_south[3] * b_south[:2]
    grad_t = grad[:2] + ADVECT * wet * flow
    grad_u = grad[2] - ADVECT * jnp.sum(wet_back[:2] * grad_x, axis=0) - latitude * wet_back[3]
    grad_v = grad[3] - ADVECT * jnp.sum(wet_back[:2] * grad_y, axis=0) + latitude * wet_back[2]

    arrived(others(own_rx), own_r)
    own = jnp.stack(exchange_blocks([own_rx[j, 0] for j in range(8)]))
    own_inter = jnp.stack(exchange_blocks([own_rx[j, 1] for j in range(8)]))
    own_dens = edge_density(own)
    start_level = (block * 8).astype(F32)
    edge_level = jnp.stack([start_level + i for i in range(8)])
    own_depth = sides(column(depth, 0), column(depth, 127))
    own_bg = sides(column(backgr, 0), column(backgr, 127))
    along = jnp.where(field == 0, lanes(own, -4), lanes(own, -2)) * sides(ADVECT, -ADVECT)
    along = jnp.where(field < 2, along, 0.0)
    own_wet = jnp.where(edge_level < own_depth, DIFFUSE, 0.0)

    arrived(halo_rx, halo_r)
    arrived(side_rx, side_r)

    def unmix(x):
        turned = rows(x, 4)
        return jnp.where(even == (row < 4), x, sides(lanes(turned, -1), lanes(turned, 1)))

    halo = unmix(jnp.stack(exchange_blocks([halo_rx[j] for j in range(8)])))
    from_west, from_east = side_rx[0], side_rx[1]
    west_depth, east_depth = column(from_west, 127), column(from_east, 0)
    inner = field < 4
    dens = jnp.where(inner, own_dens, edge_density(halo))
    depths = jnp.where(inner, own_depth, sides(east_depth, west_depth))
    backs = jnp.where(inner, own_bg, sides(column(from_east, 64), column(from_west, 63)))
    edge_wet = jnp.where(edge_level < depths, 1.0, 0.0)
    halo_wet = jnp.where(edge_level < sides(west_depth, east_depth), 1.0, 0.0)
    swapped = sides(lanes(halo, -1), lanes(halo, 1))
    delta = own_wet * (swapped - halo_wet * own) + along * swapped
    rhs = jnp.where(inner, own_inter + delta, halo)
    edge_sys, e_up, e_down = eliminate((backs + MIXING * jax.nn.sigmoid(dens[:-1] - dens[1:])) * edge_wet[1:])
    p = local_solve(edge_sys, [rhs[i] for i in range(8)])
    weight = jnp.where(start_level + 8.0 < depths, backs, 0.0)
    blocks = exchange_blocks([e_up[0], e_up[7], e_down[7], dens[0], dens[7], weight, p[0], p[7]])
    jumps = [lanes(blocks[j], -112) - lanes(blocks[j + 1], -96) for j in range(7)]
    flux = fluxes(*reduce_blocks(blocks), jumps)
    bot = jnp.where(block == 0, flux[0], 0.0)
    for j in range(1, 7):
        bot = jnp.where(block == j, lanes(flux[j], 16 * j), bot)
    top = lanes(bot, 16)
    solved = jnp.stack([p[i] + e_up[i] * top - e_down[i] * bot for i in range(8)])

    here = jnp.concatenate([solved, top[None], bot[None]], axis=0)
    for bit in (1, 2, 4):
        here = jnp.where((s & bit) != 0, lanes(here, -16 * bit), here)
    own_here = sides(here, lanes(here, -2))
    own_here = jnp.stack([lanes(own_here, -2 * f) for f in range(4)])
    after = jnp.where(edge, own_here[:, :8], after)
    top_a = jnp.where(edge, own_here[:, 8], top_a)
    bot_a = jnp.where(edge, own_here[:, 9], bot_a)
    b_edge = jnp.stack([lanes(here[:8], 119 - 2 * f) for f in range(4)])
    cols = unmix(halo_rx[s])
    cols = jnp.stack([lanes(cols, -16 * i) for i in range(8)])
    m_edge = jnp.stack([lanes(cols, 127 - 2 * f) for f in range(3)])
    beside_wet = jnp.where(jnp.logical_and(edge, level < jnp.where(last, east_depth, west_depth)), DIFFUSE * wet, 0.0)
    edge_flow = jnp.where(edge, b_edge * beside_wet, 0.0) - beside_wet * wet_back
    sign = jnp.where(last, ADVECT, jnp.where(first, -ADVECT, 0.0))
    flow = jnp.where(edge, sign * m_edge[2] * jnp.where(beside_wet > 0.0, 1.0, 0.0), 0.0)
    coef, coef_top, coef_bot = coefficients(after, top_a, bot_a)
    slope = MIXING * coef * gate * (1.0 - gate)
    slope_top = MIXING * coef_top * gate_top * (1.0 - gate_top)
    slope_bot = MIXING * coef_bot * gate_bot * (1.0 - gate_bot)
    dens_grad = wet * (
        jnp.concatenate([slope, slope_bot[None]], axis=0) - jnp.concatenate([slope_top[None], slope], axis=0)
    )
    pull = jnp.where(edge, sign * jnp.sum(wet_back[:2] * m_edge[:2], axis=0), 0.0)
    out[0] = grad_t[0] + edge_flow[0] + flow * b_edge[0] - ALPHA_T * dens_grad
    out[1] = grad_t[1] + edge_flow[1] + flow * b_edge[1] + BETA_S * dens_grad
    out[2] = grad_u + edge_flow[2] - pull
    out[3] = grad_v + edge_flow[3]

    arrived(others(part_rx), part_r)
    bg_out[...] = jnp.sum(part_rx[...], axis=0)

    @pl.when(owner)
    def _():
        arrived(others(back_rx), back_r)
        own_back = jnp.stack(exchange_blocks([back_rx[j] for j in range(8)]))
        result = jnp.sum(edge_wet[1:] * (solved[:-1] - solved[1:]) * (own_back[:-1] - own_back[1:]), axis=0)
        jump = (solved[7] - lanes(solved[0], -16)) * (own_back[7] - lanes(own_back[0], -16))
        result = result + jnp.where(weight > 0.0, jump, 0.0)
        for shift in (64, 32, 16):
            result = result + lanes(result, shift)
        result = result + lanes(result, -2)
        result = -(result + lanes(result, -4))
        bg_out[...] = jnp.where(first, result, jnp.where(last, lanes(result, 126), bg_out[...]))

        sent(back_rx.at[0], back_s)

    @pl.when(jnp.logical_not(owner))
    def _():
        sent(back_rx.at[pl.ds(0, 2)], back_s)

    sent(halo_rx, halo_s)
    sent(side_rx, side_s)
    sent(dens_rx, dens_s)
    sent(others(early_rx), early_s)
    sent(others(own_rx), own_s)
    sent(others(ret1_rx), ret1_s)
    sent(others(part_rx), part_s)


def shards(n_tile, n_store, state, cotangent, land_mask, wet_count, background):
    tile = (8, 128)
    vmem = functools.partial(pltpu.VMEM, dtype=F32)
    sem = pltpu.SemaphoreType.DMA
    n = n_store
    grad, bg_sum = pl.pallas_call(
        functools.partial(kernel, n_tile, n_store),
        name="ocean",
        out_shape=(jax.ShapeDtypeStruct(state.shape, F32), jax.ShapeDtypeStruct(tile, F32)),
        in_specs=[pl.BlockSpec(memory_space=pltpu.HBM)] * 5,
        out_specs=(pl.BlockSpec(memory_space=pltpu.VMEM), pl.BlockSpec(memory_space=pltpu.VMEM)),
        scratch_shapes=[
            vmem((2,) + state.shape), pltpu.VMEM((2,) + tile, jnp.int32), vmem(tile),
            vmem((2,) + tile), vmem(tile), vmem((2,) + tile), vmem((n,) + tile), vmem((2,) + tile), vmem((n, 2) + tile),
            vmem((2,) + tile), vmem((2,) + tile),
            vmem((n, 3) + tile), vmem((n, 3) + tile),
            vmem((n, 2) + tile), vmem((n, 2) + tile),
            vmem(tile), vmem((n,) + tile), vmem(tile), vmem((n,) + tile),
            sem((3,)),
        ] + [sem] * 16 + [pltpu.SemaphoreType.REGULAR] * 2,
        compiler_params=pltpu.CompilerParams(collective_id=0, has_side_effects=True, vmem_limit_bytes=8 << 20),
    )(*[pltpu.with_memory_space_constraint(x, pltpu.HBM) for x in (state, cotangent, land_mask, wet_count, background)])
    part = state.shape[3] // n_store
    return grad, lax.dynamic_slice_in_dim(bg_sum, lax.axis_index("store") * part, part, 1)


def solution(mesh):
    in_specs = (
        P(None, "store", None, "tile"),
        P(None, "store", None, "tile"),
        P(None, "tile"),
        P(None, "tile"),
        P(None, "tile"),
    )
    out_specs = (P(None, "store", None, "tile"), P(None, ("tile", "store")))
    body = functools.partial(shards, mesh.shape["tile"], mesh.shape["store"])
    return jax.shard_map(body, mesh=mesh, in_specs=in_specs, out_specs=out_specs, check_vma=False)
```

```python
import functools

import jax
import jax.numpy as jnp
from jax import lax
from jax.experimental import pallas as pl
from jax.experimental.pallas import tpu as pltpu
from jax.sharding import PartitionSpec as P

DIFFUSE = 0.1
ADVECT = 0.05
MIXING = 2.0
ALPHA_T = 0.6
BETA_S = 0.8
MESH = pl.DeviceIdType.MESH
F32 = jnp.float32


def lanes(x, shift):
    shift %= 128
    return pltpu.roll(x, shift, x.ndim - 1) if shift else x


def rows(x, shift):
    return pltpu.roll(x, shift % 8, x.ndim - 2)


def kernel(
    n_tile, n_store, state_h, cot_h, land_h, count_h, bg_h, out, bg_out,
    fields_in, cells_in, bg,
    xa, ya, xb, halo_rx, side_rx, own_rx, dens_tx, dens_rx,
    early, early_rx, ret1, ret1_rx, part, part_rx, back_tx, back_rx,
    in_sem, halo_s, halo_r, side_s, side_r, own_s, own_r, dens_s, dens_r,
    early_s, early_r, ret1_s, ret1_r, part_s, part_r, back_s, back_r, near, far,
):
    t = lax.axis_index("tile")
    s = lax.axis_index("store")
    east = lax.rem(t + 1, n_tile)
    west = lax.rem(t + n_tile - 1, n_tile)
    below = lax.rem(s + 1, n_store)
    above = lax.rem(s + n_store - 1, n_store)
    end = n_store - 1
    owner = jnp.logical_or(s == 0, s == end)
    late = lax.rem(t // 4, 2) == 1

    pltpu.make_async_copy(state_h, fields_in.at[0], in_sem.at[0]).start()
    pltpu.make_async_copy(cot_h, fields_in.at[1], in_sem.at[0]).start()
    pltpu.make_async_copy(land_h, cells_in.at[0], in_sem.at[1]).start()
    pltpu.make_async_copy(count_h, cells_in.at[1], in_sem.at[1]).start()
    pltpu.make_async_copy(bg_h, bg, in_sem.at[2]).start()
    st, ct = fields_in.at[0], fields_in.at[1]

    barrier = pltpu.get_barrier_semaphore()

    def greet(**where):
        pl.semaphore_signal(barrier, inc=1, device_id=where, device_id_type=MESH)

    core = lax.rem(s, 2)
    chip = s - core
    other = {"store": chip + 1 - core}
    for to in (east, west):
        for d in range(1, n_store, 2):
            greet(tile=to, store=d)
    greet(**other)
    for d in range(2, n_store, 2):
        greet(store=lax.rem(chip + d, n_store))

    lane = lax.broadcasted_iota(jnp.int32, (8, 128), 1)
    row = lax.broadcasted_iota(jnp.int32, (8, 128), 0)
    block = lane >> 4
    field = (lane & 15) >> 1
    even = (lane & 1) == 0
    pairs = ((lane + 1) & 127) >> 1
    first = lane == 0
    last = lane == 127
    edge = jnp.logical_or(first, last)

    def send(src, dst, send_sem, recv_sem, where):
        return pltpu.make_async_remote_copy(
            src_ref=src, dst_ref=dst, send_sem=send_sem, recv_sem=recv_sem, device_id=where, device_id_type=MESH
        )

    def mates(src, dst, send_sem, recv_sem):
        copies = []
        for d in range(1, n_store):
            to = lax.rem(s + d, n_store)
            copies.append(send(src(to), dst.at[s], send_sem, recv_sem, {"store": to}))
        return copies

    def arrived(ref, sem):
        send(ref, ref, sem, sem, {"tile": east}).wait_recv()

    def sent(ref, sem):
        send(ref, ref, sem, sem, {"tile": east}).wait_send()

    def others(ref):
        return ref.at[pl.ds(0, n_store - 1)]

    def start(copies):
        for copy in copies:
            copy.start()

    def exchange_blocks(tiles):
        tiles = list(tiles)
        for b in (4, 2, 1):
            keep = (block & b) == 0
            new = [None] * 8
            for v in range(8):
                if v & b == 0:
                    lo, hi = tiles[v], tiles[v + b]
                    new[v] = jnp.where(keep, lo, lanes(hi, 16 * b))
                    new[v + b] = jnp.where(keep, lanes(lo, -16 * b), hi)
            tiles = new
        return tiles

    def pack_edges(tiles, bits):
        for bit in bits:
            half = tiles.shape[0] // 2
            tiles = jnp.where((pairs & bit) != 0, lanes(tiles[half:], 2 * bit), tiles[:half])
        return tiles[0]

    def beside(x):
        return jnp.where(even, x, lanes(x, 2))

    def column(x, c):
        return jnp.broadcast_to(x[:, c : c + 1], (8, 128))

    def to_north(x):
        return jnp.where(row == 7, 0.0, rows(x, 7))

    def to_south(x):
        return jnp.where(row == 0, 0.0, rows(x, 1))

    def eliminate(mix):
        ratio, inverse = [None] * 8, [None] * 8
        above_excess = jnp.ones((8, 128), F32)
        below_excess = jnp.ones((8, 128), F32)
        for i in range(4):
            inverse[i] = 1.0 / (above_excess + mix[i])
            ratio[i] = mix[i] * inverse[i]
            above_excess = 1.0 + ratio[i] * above_excess
        for i in (7, 6, 5):
            inverse[i] = 1.0 / (below_excess + mix[i - 1])
            ratio[i] = mix[i - 1] * inverse[i]
            below_excess = 1.0 + ratio[i] * below_excess
        inverse[4] = 1.0 / (above_excess + (below_excess - 1.0))
        up, down = [None] * 8, [None] * 8
        up[0] = inverse[0]
        for i in range(1, 5):
            up[i] = mix[i - 1] * up[i - 1] * inverse[i]
        for i in (3, 2, 1, 0):
            up[i] = up[i] + ratio[i] * up[i + 1]
        for i in (5, 6, 7):
            up[i] = ratio[i] * up[i - 1]
        down[7] = inverse[7]
        for i in (6, 5, 4):
            down[i] = mix[i] * down[i + 1] * inverse[i]
        for i in (3, 2, 1, 0):
            down[i] = ratio[i] * down[i + 1]
        for i in (5, 6, 7):
            down[i] = down[i] + ratio[i] * down[i - 1]
        return (mix, ratio, inverse), up, down

    def local_solve(system, rhs):
        mix, ratio, inverse = system
        values = [None] * 8
        values[0] = rhs[0] * inverse[0]
        for i in range(1, 4):
            values[i] = (rhs[i] + mix[i - 1] * values[i - 1]) * inverse[i]
        values[7] = rhs[7] * inverse[7]
        for i in (6, 5):
            values[i] = (rhs[i] + mix[i] * values[i + 1]) * inverse[i]
        values[4] = (rhs[4] + mix[3] * values[3] + mix[4] * values[5]) * inverse[4]
        for i in (3, 2, 1, 0):
            values[i] = values[i] + ratio[i] * values[i + 1]
        for i in (5, 6, 7):
            values[i] = values[i] + ratio[i] * values[i - 1]
        return values

    def edge_density(tiles):
        dens = -ALPHA_T * tiles + BETA_S * lanes(tiles, -2)
        for bit in (1, 2, 4):
            dens = jnp.where((field & bit) == 0, dens, lanes(dens, 2 * bit))
        return dens

    def sides(a, b):
        return jnp.where(even, a, b)

    def reduce_blocks(tiles):
        rows_m, diag, lower, upper = [], [], [], []
        for j in range(7):
            here, there = tiles[j], tiles[j + 1]
            weight = lanes(here, -80)
            gates = jax.nn.sigmoid(lanes(here, -64) - lanes(there, -48))
            m = jnp.where(weight > 0.0, weight + MIXING * gates, 0.0)
            rows_m.append(m)
            diag.append(1.0 + m * (lanes(here, -32) + there))
            lower.append(m * lanes(here, -16))
            upper.append(m * lanes(there, -16))
        inv = [None] * 7

        def invert(j, pivot):
            inv[j] = 1.0 / jnp.where(block == 0, pivot, 1.0)

        invert(0, diag[0])
        invert(6, diag[6])
        for j, k in ((1, 5), (2, 4)):
            invert(j, diag[j] - lower[j] * (upper[j - 1] * inv[j - 1]))
            invert(k, diag[k] - upper[k] * (lower[k + 1] * inv[k + 1]))
        invert(3, diag[3] - lower[3] * (upper[2] * inv[2]) - upper[3] * (lower[4] * inv[4]))
        return tuple([x[j] * inv[j] for j in range(7)] for x in (rows_m, lower, upper))

    def fluxes(m_inv, low, high, jumps):
        flux = [m_inv[j] * jumps[j] for j in range(7)]
        for j, k in ((1, 5), (2, 4)):
            flux[j] = flux[j] + low[j] * flux[j - 1]
            flux[k] = flux[k] + high[k] * flux[k + 1]
        flux[3] = flux[3] + low[3] * flux[2] + high[3] * flux[4]
        for j, k in ((2, 4), (1, 5), (0, 6)):
            flux[j] = flux[j] + high[j] * flux[j + 1]
            flux[k] = flux[k] + low[k] * flux[k - 1]
        return flux

    level = (lax.broadcasted_iota(jnp.int32, (8, 8, 128), 0) + s * 8).astype(F32)
    base = (s * 8).astype(F32)

    pltpu.make_async_copy(cells_in, cells_in, in_sem.at[1]).wait()
    pltpu.make_async_copy(bg, bg, in_sem.at[2]).wait()
    pltpu.make_async_copy(fields_in, fields_in, in_sem.at[0]).wait()
    depth = jnp.where(cells_in[0] == 1, cells_in[1], 0).astype(F32)
    wet = jnp.where(level < depth, 1.0, 0.0)
    backgr = bg[...]
    masked = st[...] * wet
    fields = [masked[f] for f in range(4)] + [ct[f] for f in range(4)]
    def store_edges():
        packed = pack_edges(jnp.stack([fields[f][i] for i in range(8) for f in range(8)]), (32, 16, 8, 4, 2, 1))
        own_edges = beside(packed)

        turned = rows(own_edges, 4)
        xa[0] = sides(lanes(own_edges, -1), turned)
        xa[1] = sides(own_edges, lanes(turned, 1))
        ya[...] = jnp.where(jnp.logical_or(lane < 32, lane >= 96), depth, lanes(backgr, 64))
        xb[0] = own_edges
    pl.when(late)(store_edges)

    far_copies = []
    for side, to in enumerate((east, west)):
        for d in range(n_store):
            half = pl.ds(4 - 4 * side, 4)
            far_copies.append(
                send(xa.at[side, pl.ds(0, 4)], halo_rx.at[s, half], halo_s, halo_r, {"tile": to, "store": d})
            )
    far_copies.append(send(ya, side_rx.at[0], side_s, side_r, {"tile": east}))
    far_copies.append(send(ya, side_rx.at[1], side_s, side_r, {"tile": west}))

    def to_neighbours():
        @pl.when(core == 1)
        def _():
            pl.semaphore_wait(barrier, 2 * n_store + 1)
            pl.semaphore_signal(far, inc=1, device_id=other, device_id_type=MESH)

        @pl.when(core == 0)
        def _():
            pl.semaphore_wait(far, 1)

        start(far_copies)

    pl.when(late)(to_neighbours)

    density = -ALPHA_T * masked[0] + BETA_S * masked[1]
    dens_tx[0] = density[7]
    dens_tx[1] = density[0]
    gate = jax.nn.sigmoid(density[:-1] - density[1:])
    pair = wet[1:]
    system, up, down = eliminate((backgr + MIXING * gate) * pair)
    p_back = local_solve(system, [ct[:, i] for i in range(8)])

    shift_e = jnp.where(last, 0.0, lanes(masked, 127))
    shift_w = jnp.where(first, 0.0, lanes(masked, 1))
    around = jnp.where(level < jnp.where(last, 0.0, lanes(depth, 127)), 1.0, 0.0)
    around += jnp.where(level < jnp.where(first, 0.0, lanes(depth, 1)), 1.0, 0.0)
    around += jnp.where(level < to_north(depth), 1.0, 0.0)
    around += jnp.where(level < to_south(depth), 1.0, 0.0)
    centre = wet * (1.0 - DIFFUSE * around)
    spread = DIFFUSE * wet
    m_north = to_north(masked)
    m_south = to_south(masked)
    latitude = 0.1 + 0.2 * (row.astype(F32) + 0.5) / 8.0
    inter = centre * masked + spread * (shift_e + shift_w + m_north + m_south)
    zonal, merid = masked[2], masked[3]
    grad_x = shift_e[:2] - shift_w[:2]
    grad_y = m_north[:2] - m_south[:2]
    advect = -ADVECT * (zonal * grad_x + merid * grad_y)
    inter = [inter[0] + advect[0], inter[1] + advect[1], inter[2] + latitude * merid, inter[3] - latitude * zonal]
    inter_edges = [inter[f][i] for i in range(8) for f in range(4)]
    inter = jnp.stack(inter)
    p_after = local_solve(system, [inter[:, i] for i in range(8)])

    bottom_wet = base + 8.0 < depth
    bg_pair = jnp.where(bottom_wet, backgr, 0.0)
    groups = (
        [p_back[0][f] for f in range(4)] + [p_back[7][f] for f in range(4)],
        [p_after[0][f] for f in range(4)] + [p_after[7][f] for f in range(4)],
        [up[0], up[7], down[7], density[0], density[7], bg_pair, bg_pair, bg_pair],
    )
    for g, group in enumerate(groups):
        for d, tile in enumerate(exchange_blocks(group)):
            early[d, g] = tile
    early_rx[s] = early[s]

    @pl.when(core == 0)
    def _():
        pl.semaphore_wait(barrier, end)
        pl.semaphore_signal(near, inc=1, device_id=other, device_id_type=MESH)

    @pl.when(core == 1)
    def _():
        pl.semaphore_wait(near, 1)

    early_copies = mates(lambda to: early.at[to], early_rx, early_s, early_r)
    start(early_copies)
    dens_copies = [
        send(dens_tx.at[0], dens_rx.at[0], dens_s, dens_r, {"store": below}),
        send(dens_tx.at[1], dens_rx.at[1], dens_s, dens_r, {"store": above}),
    ]
    start(dens_copies)
    pl.when(jnp.logical_not(late))(store_edges)
    xb[1] = beside(pack_edges(jnp.stack(inter_edges), (32, 16, 8, 2, 1)))
    own_rx[s] = xb[...]
    own_copies = mates(lambda to: xb, own_rx, own_s, own_r)
    start(own_copies)

    arrived(others(early_rx), early_r)
    coefs = reduce_blocks([early_rx[j, 2] for j in range(8)])

    def four(x):
        x = jnp.where(block == 0, x, lanes(x, 16))
        return jnp.where(block < 2, x, lanes(x, 32))

    coefs = [[four(x) for x in xs] for xs in coefs]
    left = lane < 64
    for g in range(2):
        ends = [early_rx[j, g] for j in range(8)]
        flux = fluxes(*coefs, [lanes(ends[j], 64) - ends[j + 1] for j in range(7)])
        for d in range(8):
            above_flux = flux[d - 1] if d else 0.0
            below_flux = lanes(flux[d], 64) if d < 7 else 0.0
            ret1[d, g] = jnp.where(left, above_flux, below_flux)
    ret1_rx[s] = ret1[s]
    ret1_copies = mates(lambda to: ret1.at[to], ret1_rx, ret1_s, ret1_r)
    start(ret1_copies)
    pl.when(jnp.logical_not(late))(to_neighbours)

    arrived(dens_rx, dens_r)
    gate_top = jax.nn.sigmoid(dens_rx[0] - density[0])
    gate_bot = jax.nn.sigmoid(density[7] - dens_rx[1])
    pair_top = jnp.where(base > 0.0, wet[0], 0.0)
    pair_bot = jnp.where(bottom_wet, 1.0, 0.0)
    scale_top = pair_top / (backgr + MIXING * gate_top)
    scale_bot = pair_bot / (backgr + MIXING * gate_bot)

    def coefficients(after, top_a, bot_a):
        coef = -jnp.sum(diff_b * (after[:, :-1] - after[:, 1:]), axis=0) * pair
        coef_top = -jnp.sum(top_b * top_a, axis=0) * (scale_top * scale_top)
        coef_bot = -jnp.sum(bot_b * bot_a, axis=0) * (scale_bot * scale_bot)
        return coef, coef_top, coef_bot

    def finish(p, top, bot):
        return jnp.stack([p[i] + up[i] * top - down[i] * bot for i in range(8)], axis=1)

    arrived(others(ret1_rx), ret1_r)
    flux_b = exchange_blocks([ret1_rx[d, 0] for d in range(8)])
    flux_a = exchange_blocks([ret1_rx[d, 1] for d in range(8)])
    top_b, bot_b = jnp.stack(flux_b[:4]), jnp.stack(flux_b[4:])
    top_a, bot_a = jnp.stack(flux_a[:4]), jnp.stack(flux_a[4:])
    back = finish(p_back, top_b, bot_b)
    diff_b = back[:, :-1] - back[:, 1:]
    after = finish(p_after, top_a, bot_a)
    coef, _, coef_bot = coefficients(after, top_a, bot_a)
    total = jnp.sum(coef, axis=0) + coef_bot
    part[...] = total
    part_rx[s] = total
    part_copies = mates(lambda to: part, part_rx, part_s, part_r)
    start(part_copies)
    wet_back = wet * back
    back_tx[...] = beside(pack_edges(jnp.stack([back[f, i] for i in range(8) for f in range(4)]), (32, 16, 8, 2, 1)))
    back_rx[s] = back_tx[...]
    back_copies = [
        (to, send(back_tx, back_rx.at[s], back_s, back_r, {"store": to})) for to in (0, end)
    ]
    for to, copy in back_copies:
        pl.when(s != to)(copy.start)


    b_east = jnp.where(last, 0.0, lanes(wet_back, 127))
    b_west = jnp.where(first, 0.0, lanes(wet_back, 1))
    b_north = to_north(wet_back)
    b_south = to_south(wet_back)
    grad = centre * wet_back + spread * (b_east + b_west + b_north + b_south)
    flow = shift_e[2] * b_east[:2] - shift_w[2] * b_west[:2] + m_north[3] * b_north[:2] - m_south[3] * b_south[:2]
    grad_t = grad[:2] + ADVECT * wet * flow
    grad_u = grad[2] - ADVECT * jnp.sum(wet_back[:2] * grad_x, axis=0) - latitude * wet_back[3]
    grad_v = grad[3] - ADVECT * jnp.sum(wet_back[:2] * grad_y, axis=0) + latitude * wet_back[2]

    arrived(others(own_rx), own_r)
    own = jnp.stack(exchange_blocks([own_rx[j, 0] for j in range(8)]))
    own_inter = jnp.stack(exchange_blocks([own_rx[j, 1] for j in range(8)]))
    own_dens = edge_density(own)
    start_level = (block * 8).astype(F32)
    edge_level = jnp.stack([start_level + i for i in range(8)])
    own_depth = sides(column(depth, 0), column(depth, 127))
    own_bg = sides(column(backgr, 0), column(backgr, 127))
    along = jnp.where(field == 0, lanes(own, -4), lanes(own, -2)) * sides(ADVECT, -ADVECT)
    along = jnp.where(field < 2, along, 0.0)
    own_wet = jnp.where(edge_level < own_depth, DIFFUSE, 0.0)

    arrived(halo_rx, halo_r)
    arrived(side_rx, side_r)

    def unmix(x):
        turned = rows(x, 4)
        return jnp.where(even == (row < 4), x, sides(lanes(turned, -1), lanes(turned, 1)))

    halo = unmix(jnp.stack(exchange_blocks([halo_rx[j] for j in range(8)])))
    from_west, from_east = side_rx[0], side_rx[1]
    west_depth, east_depth = column(from_west, 127), column(from_east, 0)
    inner = field < 4
    dens = jnp.where(inner, own_dens, edge_density(halo))
    depths = jnp.where(inner, own_depth, sides(east_depth, west_depth))
    backs = jnp.where(inner, own_bg, sides(column(from_east, 64), column(from_west, 63)))
    edge_wet = jnp.where(edge_level < depths, 1.0, 0.0)
    halo_wet = jnp.where(edge_level < sides(west_depth, east_depth), 1.0, 0.0)
    swapped = sides(lanes(halo, -1), lanes(halo, 1))
    delta = own_wet * (swapped - halo_wet * own) + along * swapped
    rhs = jnp.where(inner, own_inter + delta, halo)
    edge_sys, e_up, e_down = eliminate((backs + MIXING * jax.nn.sigmoid(dens[:-1] - dens[1:])) * edge_wet[1:])
    p = local_solve(edge_sys, [rhs[i] for i in range(8)])
    weight = jnp.where(start_level + 8.0 < depths, backs, 0.0)
    blocks = exchange_blocks([e_up[0], e_up[7], e_down[7], dens[0], dens[7], weight, p[0], p[7]])
    jumps = [lanes(blocks[j], -112) - lanes(blocks[j + 1], -96) for j in range(7)]
    flux = fluxes(*reduce_blocks(blocks), jumps)
    bot = jnp.where(block == 0, flux[0], 0.0)
    for j in range(1, 7):
        bot = jnp.where(block == j, lanes(flux[j], 16 * j), bot)
    top = lanes(bot, 16)
    solved = jnp.stack([p[i] + e_up[i] * top - e_down[i] * bot for i in range(8)])

    here = jnp.concatenate([solved, top[None], bot[None]], axis=0)
    for bit in (1, 2, 4):
        here = jnp.where((s & bit) != 0, lanes(here, -16 * bit), here)
    own_here = sides(here, lanes(here, -2))
    own_here = jnp.stack([lanes(own_here, -2 * f) for f in range(4)])
    after = jnp.where(edge, own_here[:, :8], after)
    top_a = jnp.where(edge, own_here[:, 8], top_a)
    bot_a = jnp.where(edge, own_here[:, 9], bot_a)
    b_edge = jnp.stack([lanes(here[:8], 119 - 2 * f) for f in range(4)])
    cols = unmix(halo_rx[s])
    cols = jnp.stack([lanes(cols, -16 * i) for i in range(8)])
    m_edge = jnp.stack([lanes(cols, 127 - 2 * f) for f in range(3)])
    beside_wet = jnp.where(jnp.logical_and(edge, level < jnp.where(last, east_depth, west_depth)), DIFFUSE * wet, 0.0)
    edge_flow = jnp.where(edge, b_edge * beside_wet, 0.0) - beside_wet * wet_back
    sign = jnp.where(last, ADVECT, jnp.where(first, -ADVECT, 0.0))
    flow = jnp.where(edge, sign * m_edge[2] * jnp.where(beside_wet > 0.0, 1.0, 0.0), 0.0)
    coef, coef_top, coef_bot = coefficients(after, top_a, bot_a)
    slope = MIXING * coef * gate * (1.0 - gate)
    slope_top = MIXING * coef_top * gate_top * (1.0 - gate_top)
    slope_bot = MIXING * coef_bot * gate_bot * (1.0 - gate_bot)
    dens_grad = wet * (
        jnp.concatenate([slope, slope_bot[None]], axis=0) - jnp.concatenate([slope_top[None], slope], axis=0)
    )
    pull = jnp.where(edge, sign * jnp.sum(wet_back[:2] * m_edge[:2], axis=0), 0.0)
    out[0] = grad_t[0] + edge_flow[0] + flow * b_edge[0] - ALPHA_T * dens_grad
    out[1] = grad_t[1] + edge_flow[1] + flow * b_edge[1] + BETA_S * dens_grad
    out[2] = grad_u + edge_flow[2] - pull
    out[3] = grad_v + edge_flow[3]

    arrived(others(part_rx), part_r)
    total = jnp.sum(part_rx[...], axis=0)
    for bit in (1, 2, 4):
        total = jnp.where((s & bit) != 0, lanes(total, -16 * bit), total)
    bg_out[...] = total

    @pl.when(owner)
    def _():
        arrived(others(back_rx), back_r)
        own_back = jnp.stack(exchange_blocks([back_rx[j] for j in range(8)]))
        result = jnp.sum(edge_wet[1:] * (solved[:-1] - solved[1:]) * (own_back[:-1] - own_back[1:]), axis=0)
        jump = (solved[7] - lanes(solved[0], -16)) * (own_back[7] - lanes(own_back[0], -16))
        result = result + jnp.where(weight > 0.0, jump, 0.0)
        for shift in (64, 32, 16):
            result = result + lanes(result, shift)
        result = result + lanes(result, -2)
        result = -(result + lanes(result, -4))
        at_west = jnp.logical_and(first, s == 0)
        at_east = jnp.logical_and(lane == 15, s == end)
        bg_out[...] = jnp.where(at_west, result, jnp.where(at_east, lanes(result, 14), bg_out[...]))

        sent(back_rx.at[0], back_s)

    @pl.when(jnp.logical_not(owner))
    def _():
        sent(back_rx.at[pl.ds(0, 2)], back_s)

    sent(halo_rx, halo_s)
    sent(side_rx, side_s)
    sent(dens_rx, dens_s)
    sent(others(early_rx), early_s)
    sent(others(own_rx), own_s)
    sent(others(ret1_rx), ret1_s)
    sent(others(part_rx), part_s)


def write_out(grad, bg_sum, out, bg_out, held, out_sem, bg_sem):
    copy = pltpu.make_async_copy(grad, out, out_sem)
    copy.start()
    held[...] = bg_sum[:, :16]
    bg_copy = pltpu.make_async_copy(held, bg_out, bg_sem)
    bg_copy.start()
    copy.wait()
    bg_copy.wait()


def shards(n_tile, n_store, state, cotangent, land_mask, wet_count, background):
    tile = (8, 128)
    vmem = functools.partial(pltpu.VMEM, dtype=F32)
    sem = pltpu.SemaphoreType.DMA
    n = n_store
    grad, bg_sum = pl.pallas_call(
        functools.partial(kernel, n_tile, n_store),
        name="ocean",
        out_shape=(jax.ShapeDtypeStruct(state.shape, F32), jax.ShapeDtypeStruct(tile, F32)),
        in_specs=[pl.BlockSpec(memory_space=pltpu.HBM)] * 5,
        out_specs=(pl.BlockSpec(memory_space=pltpu.VMEM), pl.BlockSpec(memory_space=pltpu.VMEM)),
        scratch_shapes=[
            vmem((2,) + state.shape), pltpu.VMEM((2,) + tile, jnp.int32), vmem(tile),
            vmem((2,) + tile), vmem(tile), vmem((2,) + tile), vmem((n,) + tile), vmem((2,) + tile), vmem((n, 2) + tile),
            vmem((2,) + tile), vmem((2,) + tile),
            vmem((n, 3) + tile), vmem((n, 3) + tile),
            vmem((n, 2) + tile), vmem((n, 2) + tile),
            vmem(tile), vmem((n,) + tile), vmem(tile), vmem((n,) + tile),
            sem((3,)),
        ] + [sem] * 16 + [pltpu.SemaphoreType.REGULAR] * 2,
        compiler_params=pltpu.CompilerParams(collective_id=0, has_side_effects=True, vmem_limit_bytes=8 << 20),
    )(*[pltpu.with_memory_space_constraint(x, pltpu.HBM) for x in (state, cotangent, land_mask, wet_count, background)])
    columns = jax.ShapeDtypeStruct((8, state.shape[3] // n_store), F32)
    return pl.pallas_call(
        write_out,
        name="write_out",
        out_shape=(jax.ShapeDtypeStruct(state.shape, F32), columns),
        in_specs=[pl.BlockSpec(memory_space=pltpu.VMEM)] * 2,
        out_specs=(pl.BlockSpec(memory_space=pl.ANY), pl.BlockSpec(memory_space=pl.ANY)),
        scratch_shapes=[vmem(columns.shape), sem, sem],
        compiler_params=pltpu.CompilerParams(vmem_limit_bytes=8 << 20),
    )(grad, bg_sum)


def solution(mesh):
    in_specs = (
        P(None, "store", None, "tile"),
        P(None, "store", None, "tile"),
        P(None, "tile"),
        P(None, "tile"),
        P(None, "tile"),
    )
    out_specs = (P(None, "store", None, "tile"), P(None, ("tile", "store")))
    body = functools.partial(shards, mesh.shape["tile"], mesh.shape["store"])
    return jax.shard_map(body, mesh=mesh, in_specs=in_specs, out_specs=out_specs, check_vma=False)
```
